256 devices in a mesh: bl: 64 (over y, z, core), ch: 4 (over x).
Axes of the slice: x: 4, y: 4, z: 8, core: 2. Of those that a mesh axis runs over, the one named last changes fastest.
Arguments:
- facet_grid: bfloat16 [4, 64, 16, 1024], P(None, None, None, 'ch'), may hold values from -0.75 to 0.75
- kernel: bfloat16 [131072, 1024], P('bl', 'ch'), may hold values from -0.1875 to 0.1875
- tile_of: int32 [256], P('bl'), may hold values from 0 to 3
- observed: bfloat16 [64, 2, 131072], P('ch', None, 'bl'), may hold values from -6 to 6
- flags: int32 [64, 131072], P('ch', 'bl'), may hold values 0 or 1
- pairs: int32 [2, 131072], P(None, 'bl'), may hold values from 0 to 511, as said below
- solver_order: int32 [512], replicated, may hold values from 0 to 511, as said below
Outputs:
- gains: float32 [64, 16, 512], P('ch', None, 'bl')
The draws below stay inside these ranges and needn't reach their ends.
Inputs may be any that keep to these rules, and one draw needn't show every extreme that they name: `solver_order`: each station appears once. `pairs`: for row r, with j = (r mod 2048) // 32, the first station is solver_order[8 * j + m] for some m below 8; the second station differs from the first.
All inputs are finite; a program needn't handle non-finite values. No bound on the sum of `flags` on one device may be relied on, other than what follows from the above.
Results may differ from the reference program's by a relative error of at most 0.013.
Values may be sent and summed in bfloat16 or wider, within the bound.
No kernel may reach another device: no remote copies, remote signals or barrier semaphores. Data moves between devices by JAX's collectives and lax.ppermute only.
A program may use at most 128 MiB of HBM per device.

```python
import jax
import jax.numpy as jnp
from jax import lax

S = 512
ND = 8
TILE = 1024
NTILE = 4
BLK = 512
ITERS = 4
VIS_DEV = 2048
NCH = 64
NVIS = 131072
S_DEV = 8
SEG = 32
N_CH = 4


def order_of(key):
    return jax.random.permutation(jax.random.fold_in(key, 11), S).astype(jnp.int32)


def draw_solver_order(key, part):
    return order_of(key)


def draw_pairs(key, part):
    station_order = order_of(key)
    row_index = jnp.arange(NVIS, dtype=jnp.int32)
    segment = row_index % VIS_DEV // SEG
    within = jax.random.randint(jax.random.fold_in(key, 12), (NVIS,), 0, S_DEV, dtype=jnp.int32)
    first_station = station_order[segment * S_DEV + within]
    offset = jax.random.randint(jax.random.fold_in(key, 13), (NVIS,), 1, S, dtype=jnp.int32)
    second_station = (first_station + offset) % S
    return jnp.stack([first_station, second_station]).astype(jnp.int32)


def touch_ends(drawn, own_key, least, largest):
    longest = drawn.shape.index(max(drawn.shape))
    spots = []
    for shift in (0, 1):
        where = [jax.random.randint(jax.random.fold_in(own_key, axis), (), 0, length) for axis, length in enumerate(drawn.shape)]
        where[longest] = (where[longest] + shift) % drawn.shape[longest]
        spots.append(tuple(where))
    return drawn.at[spots[0]].set(least).at[spots[1]].set(largest)


def steps_of(key, shape, shards, smallest, top_value):
    def one(position, shards_of):
        steps = jax.random.uniform(jax.random.fold_in(jax.random.fold_in(key, 6), position), (shards_of,), jnp.float32, smallest / len(shards), top_value / len(shards))
        return jnp.repeat(jnp.exp(steps), shape[position] // shards_of).reshape((-1,) + (1,) * (len(shape) - position - 1))

    level = one(*shards[0])
    for cut in shards[1:]:
        level = level * one(*cut)
    return level


def noise(rng, dims, spread, bound, pieces=(), kind=jnp.bfloat16):
    loudness = steps_of(rng, dims, pieces, -0.22, 0.18) if pieces else 1.0
    values = jax.random.normal(rng, dims, jnp.float32) * spread * loudness
    return jnp.minimum(jnp.maximum(values, -bound), bound).astype(kind)


def setup_inputs(seed: int = 0) -> dict:
    keys = jax.random.split(jax.random.key(seed), 8)
    facet_grid = noise(keys[0], (NTILE, NCH, 2 * ND, TILE), (0.8 * (NVIS // S) ** -0.5), 0.75, ((3, 4),))
    kernel = noise(keys[1], (NVIS, TILE), TILE ** -0.5, 0.1875, ((0, 64), (1, 4)))
    tile_of = touch_ends(jax.random.randint(keys[2], (NVIS // BLK,), 0, NTILE), jax.random.fold_in(keys[2], 1), 0, NTILE - 1).astype(jnp.int32)
    observed = noise(keys[3], (NCH, 2, NVIS), 1.0, 6.0, ((0, 4), (2, 64)))
    flags = touch_ends((jax.random.randint(keys[4], (NCH, NVIS), 0, 8) < 1).astype(jnp.int32), jax.random.fold_in(keys[4], 1), 0, 1)
    pairs = draw_pairs(jax.random.fold_in(keys[7], 71), 0)
    solver_order = draw_solver_order(jax.random.fold_in(keys[7], 71), 0)
    return dict(facet_grid=facet_grid, kernel=kernel, tile_of=tile_of, observed=observed, flags=flags, pairs=pairs, solver_order=solver_order)


def degrid(facet_grid, kernel, tile_of):
    group_width = TILE // N_CH
    kernel_blocks = kernel.reshape(NVIS // BLK, BLK, N_CH, group_width)

    def one_block(inputs):
        tile_index, block_kernel = inputs
        tile_cells = facet_grid[tile_index].astype(jnp.float32).reshape(NCH, 2 * ND, N_CH, group_width)
        group_sums = jnp.einsum('ckgu,vgu->gckv', tile_cells, block_kernel.astype(jnp.float32))
        rounded = lax.optimization_barrier(group_sums.astype(jnp.bfloat16)).astype(jnp.float32)
        return jnp.sum(rounded, axis=0)

    blocks = lax.map(one_block, (tile_of, kernel_blocks))
    return jnp.transpose(blocks, (1, 2, 0, 3)).reshape(NCH, 2 * ND, NVIS)


def channel_sums(inputs, first_slot, second_slot):
    model_row, visible_row, gain_row = inputs
    model_pair = model_row.astype(jnp.float32).reshape(ND, 2, NVIS)
    gain_pair = gain_row.reshape(ND, 2, S)
    model_re = model_pair[:, 0]
    model_im = model_pair[:, 1]
    far_re = gain_pair[:, 0][:, second_slot]
    far_im = gain_pair[:, 1][:, second_slot]
    near_re = gain_pair[:, 0][:, first_slot]
    near_im = gain_pair[:, 1][:, first_slot]
    prod_re = model_re * far_re + model_im * far_im
    prod_im = model_im * far_re - model_re * far_im
    pred_re = jnp.sum(near_re * prod_re - near_im * prod_im, axis=0)
    pred_im = jnp.sum(near_re * prod_im + near_im * prod_re, axis=0)
    vis_pair = visible_row.astype(jnp.float32)
    resid_re = vis_pair[0] - pred_re
    resid_im = vis_pair[1] - pred_im
    empty = jnp.zeros((ND, S), jnp.float32)
    sum_re = empty.at[:, first_slot].add(prod_re * resid_re + prod_im * resid_im)
    sum_im = empty.at[:, first_slot].add(prod_re * resid_im - prod_im * resid_re)
    power = empty.at[:, first_slot].add(prod_re * prod_re + prod_im * prod_im)
    return sum_re, sum_im, power


def reference(facet_grid, kernel, tile_of, observed, flags, pairs, solver_order):
    kept = (1 - flags).astype(jnp.float32)
    model_vis = (degrid(facet_grid, kernel, tile_of) * kept[:, None, :]).astype(jnp.bfloat16)
    visible = (observed.astype(jnp.float32) * kept[:, None, :]).astype(jnp.bfloat16)
    inverse = jnp.zeros((S,), jnp.int32).at[solver_order].set(jnp.arange(S, dtype=jnp.int32))
    first_slot = inverse[pairs[0]].astype(jnp.int32)
    second_slot = inverse[pairs[1]].astype(jnp.int32)
    gains = jnp.zeros((NCH, ND, 2, S), jnp.float32).at[:, :, 0, :].set(1.0).reshape(NCH, 2 * ND, S)
    has_left = (jnp.arange(NCH) > 0).astype(jnp.float32)[:, None, None]
    has_right = (jnp.arange(NCH) < NCH - 1).astype(jnp.float32)[:, None, None]
    for iteration in range(ITERS):
        sum_re, sum_im, power = lax.map(lambda inputs: channel_sums(inputs, first_slot, second_slot), (model_vis, visible, gains))
        gain_pair = gains.reshape(NCH, ND, 2, S)
        gain_re = gain_pair[:, :, 0]
        gain_im = gain_pair[:, :, 1]
        new_re = (sum_re + gain_re * power) / (power + 1.0)
        new_im = (sum_im + gain_im * power) / (power + 1.0)
        averaged = jnp.stack([(gain_re + new_re) * 0.5, (gain_im + new_im) * 0.5], axis=2).reshape(NCH, 2 * ND, S)
        padded = jnp.pad(averaged, ((1, 1), (0, 0), (0, 0)))
        gains = (0.25 * has_left * padded[:-2] + 0.5 * padded[1:-1] + 0.25 * has_right * padded[2:]) / (0.5 + 0.25 * has_left + 0.25 * has_right)
    return gains
```

```python
import jax
import jax.numpy as jnp
from jax import lax
from jax.experimental import pallas as pl
from jax.experimental.pallas import tpu as pltpu
from jax.sharding import PartitionSpec as P

S = 512
ND = 8
ITERS = 4
LANES = 128
ROWS = 2048
HALF = 1024
BLK = 512
CHUNK = 256
F32 = jnp.float32
BF16 = jnp.bfloat16


def nt(a, b):
    return lax.dot_general(a, b, (((1,), (1,)), ((), ())), preferred_element_type=F32)


def nn(a, b):
    return lax.dot_general(a, b, (((1,), (0,)), ((), ())), preferred_element_type=F32)


def iota(shape, dim):
    return lax.broadcasted_iota(jnp.int32, shape, dim)


def lane_order():
    lane = iota((256, 256), 0)
    source = (lane & 15) * 16 + ((lane >> 4) & 7) * 2 + (lane >> 7)
    return (iota((256, 256), 1) == source).astype(F32).astype(BF16)


def degrid_kernel(groups):
    def run(where_ref, tile_ref, kern_ref, facet_ref, *outs):
        order = lane_order()
        here = where_ref[0]
        for block in range(4):
            rows = kern_ref[block * BLK : (block + 1) * BLK, :]
            tile = tile_ref[block]
            for index, shift in enumerate(groups):
                first = ((here + shift) & 3) * 16
                facet = facet_ref[tile, pl.ds(first, 16)].reshape(256, 256)
                facet = nn(order, facet).astype(BF16)
                out = outs[2 * index + block // 2]
                start = (block % 2) * BLK
                out[start : start + BLK, :] = nt(rows, facet).astype(BF16)

    return run


def degrid(where, tile_of, kernel, facet_grid, groups):
    smem = pl.BlockSpec(memory_space=pltpu.SMEM)
    vmem = pl.BlockSpec(memory_space=pltpu.VMEM)
    return pl.pallas_call(
        degrid_kernel(groups),
        out_shape=[jax.ShapeDtypeStruct((HALF, 256), BF16)] * (2 * len(groups)),
        in_specs=[smem, smem, vmem, vmem],
        out_specs=[vmem] * (2 * len(groups)),
        name="degrid%d" % len(groups),
    )(where, tile_of, kernel, facet_grid)


def payload_kernel(obs_ref, flag_ref, pair_ref, out_ref):
    kept = (1 - flag_ref[...]).astype(F32)
    pair = pair_ref[...]
    high = (pair >> 3).astype(F32)
    low = (pair & 7).astype(F32)
    fill = jnp.zeros((LANES - 52, ROWS), F32)
    stacked = jnp.concatenate([obs_ref[...].astype(F32), kept, high, low, fill], axis=0)
    for part in range(ROWS // 128):
        out_ref[part * 128 : (part + 1) * 128, :] = stacked[:, part * 128 : (part + 1) * 128].T.astype(BF16)


def make_payload(observed, flags, pairs):
    return pl.pallas_call(
        payload_kernel,
        out_shape=jax.ShapeDtypeStruct((ROWS, LANES), BF16),
        name="payload",
    )(observed.reshape(32, ROWS), flags, pairs)


def setup_kernel(pay_ref, order_ref, own_ref, ohq_ref, ohp_ref, opt_ref, vre_ref, vim_ref, kept_ref):
    source = iota((LANES, 5 * LANES), 0)
    col = iota((LANES, 5 * LANES), 1)
    piece = col >> 7
    chan = col & 15
    spread = (source == 2 * chan + piece) & (piece < 2)
    spread = spread | ((source == 32 + chan) & (piece == 2))
    weight = spread.astype(F32)
    weight = weight + 8.0 * ((source == 49) & (piece == 3)).astype(F32) + ((source == 51) & (piece == 3)).astype(F32)
    weight = weight + 8.0 * ((source == 48) & (piece == 4)).astype(F32) + ((source == 50) & (piece == 4)).astype(F32)
    weight = weight.astype(BF16)
    order = order_ref[...]
    own = own_ref[...]

    def step(i, carry):
        rows = pl.ds(pl.multiple_of(i * CHUNK, CHUNK), CHUNK)
        wide = nn(pay_ref[rows, :], weight)
        kept = wide[:, 256:384]
        vre_ref[rows, :] = wide[:, :128] * kept
        vim_ref[rows, :] = wide[:, 128:256] * kept
        kept_ref[rows, :] = kept
        second = wide[:, 384:512]
        first = wide[:, 512:640]
        for part in range(4):
            lanes = slice(part * 128, (part + 1) * 128)
            ohq_ref[rows, lanes] = (second == order[:, lanes]).astype(F32).astype(BF16)
        near = (first == own).astype(F32)
        ohp_ref[rows, :] = near.astype(BF16)
        opt_ref[:, rows] = near.T[:16, :].astype(BF16)
        return carry

    lax.fori_loop(0, ROWS // CHUNK, step, 0)


def make_setup(payload, order, own):
    shapes = [
        jax.ShapeDtypeStruct((ROWS, S), BF16),
        jax.ShapeDtypeStruct((ROWS, LANES), BF16),
        jax.ShapeDtypeStruct((16, ROWS), BF16),
        jax.ShapeDtypeStruct((ROWS, LANES), F32),
        jax.ShapeDtypeStruct((ROWS, LANES), F32),
        jax.ShapeDtypeStruct((ROWS, LANES), F32),
    ]
    return pl.pallas_call(setup_kernel, out_shape=shapes, name="setup")(payload, order, own)


def over_directions(x):
    x = x + pltpu.roll(x, 16, 1)
    x = x + pltpu.roll(x, 32, 1)
    return x + pltpu.roll(x, 64, 1)


def iterate_kernel(first):
    def run(*refs):
        if first:
            model_ref, opt_ref, vre_ref, vim_ref, kept_ref, out_ref = refs
        else:
            model_ref, opt_ref, vre_ref, vim_ref, kept_ref, ohq_ref, ohp_ref, all_ref, own_ref, out_ref = refs
            all_gains = all_ref[...]
            own = own_ref[...]
            high = own.astype(BF16).astype(F32)
            near_gains = jnp.concatenate([high, own - high, jnp.zeros((LANES - 16, 256), F32)], axis=0).astype(BF16)

        def step(i, acc):
            rows = pl.ds(pl.multiple_of(i * CHUNK, CHUNK), CHUNK)
            kept = kept_ref[rows, :]
            model_re = model_ref[rows, :128].astype(F32) * kept
            model_im = model_ref[rows, 128:].astype(F32) * kept
            if first:
                prod_re = pred_re = model_re
                prod_im = pred_im = model_im
            else:
                far = nn(ohq_ref[rows, :], all_gains)
                near = nn(ohp_ref[rows, :], near_gains)
                far_re, far_im = far[:, :128], far[:, 128:]
                near_re, near_im = near[:, :128], near[:, 128:]
                prod_re = model_re * far_re + model_im * far_im
                prod_im = model_im * far_re - model_re * far_im
                pred_re = near_re * prod_re - near_im * prod_im
                pred_im = near_re * prod_im + near_im * prod_re
            res_re = vre_ref[rows, :] - over_directions(pred_re)
            res_im = vim_ref[rows, :] - over_directions(pred_im)
            terms = jnp.concatenate(
                [
                    prod_re * res_re + prod_im * res_im,
                    prod_re * res_im - prod_im * res_re,
                    prod_re * prod_re + prod_im * prod_im,
                ],
                axis=1,
            )
            top = terms.astype(BF16)
            rest = (terms - top.astype(F32)).astype(BF16)
            pick = opt_ref[:, rows]
            return acc + nn(pick, top) + nn(pick, rest)

        acc = lax.fori_loop(0, ROWS // CHUNK, step, jnp.zeros((16, 384), F32))[:8]
        sum_re, sum_im, power = acc[:, :128], acc[:, 128:256], acc[:, 256:]
        if first:
            gain_re = jnp.ones((8, 128), F32)
            gain_im = jnp.zeros((8, 128), F32)
        else:
            gain_re, gain_im = own[:, :128], own[:, 128:]
        new_re = (sum_re + gain_re * power) / (power + 1.0)
        new_im = (sum_im + gain_im * power) / (power + 1.0)
        out_ref[:, :128] = (gain_re + new_re) * 0.5
        out_ref[:, 128:] = (gain_im + new_im) * 0.5

    return run


def iterate(args, first):
    return pl.pallas_call(
        iterate_kernel(first),
        out_shape=jax.ShapeDtypeStruct((8, 256), F32),
        name="iterate0" if first else "iterate",
    )(*args)


def smooth_kernel(spread):
    def run(where_ref, mid_ref, low_ref, high_ref, out_ref, *more):
        chan = iota((8, LANES), 1) & 15
        whole = chan + 16 * where_ref[0]
        has_left = (whole > 0).astype(F32)
        has_right = (whole < 63).astype(F32)
        for part in range(2):
            lanes = slice(part * 128, (part + 1) * 128)
            mid = mid_ref[:, lanes]
            left = jnp.where(chan == 0, pltpu.roll(low_ref[:, lanes], 113, 1), pltpu.roll(mid, 1, 1))
            right = jnp.where(chan == 15, pltpu.roll(high_ref[:, lanes], 15, 1), pltpu.roll(mid, 127, 1))
            total = 0.25 * has_left * left + 0.5 * mid + 0.25 * has_right * right
            out_ref[:, lanes] = total / (0.5 + 0.25 * has_left + 0.25 * has_right)
        if spread:
            more[0][...] = jnp.broadcast_to(out_ref[...].astype(BF16)[None], (64, 8, 256))

    return run


def smooth(where, mid, low, high, spread):
    shapes = [jax.ShapeDtypeStruct((8, 256), F32)]
    if spread:
        shapes.append(jax.ShapeDtypeStruct((64, 8, 256), BF16))
    smem = pl.BlockSpec(memory_space=pltpu.SMEM)
    vmem = pl.BlockSpec(memory_space=pltpu.VMEM)
    return pl.pallas_call(
        smooth_kernel(spread),
        out_shape=shapes,
        in_specs=[smem, vmem, vmem, vmem],
        out_specs=[vmem] * len(shapes),
        name="smooth",
    )(where, mid, low, high)


def add_kernel(own_a, own_b, chain_a, chain_b, near_a, near_b, out_ref):
    out_ref[:HALF, :] = (own_a[...].astype(F32) + chain_a[...].astype(F32) + near_a[...].astype(F32)).astype(BF16)
    out_ref[HALF:, :] = (own_b[...].astype(F32) + chain_b[...].astype(F32) + near_b[...].astype(F32)).astype(BF16)


def body(facet_grid, kernel, tile_of, observed, flags, pairs, solver_order):
    where = lax.axis_index("ch").astype(jnp.int32).reshape(1)
    up = [(i, (i + 1) % 4) for i in range(4)]
    down = [(i, (i + 3) % 4) for i in range(4)]

    far_a, far_b = degrid(where, tile_of, kernel, facet_grid, (2,))
    chain_a = lax.ppermute(far_a, "ch", up)
    chain_b = lax.ppermute(far_b, "ch", down)
    next_a, next_b, prev_a, prev_b, own_a, own_b = degrid(where, tile_of, kernel, facet_grid, (1, 3, 0))
    direct_a = lax.ppermute(prev_a, "ch", down)
    direct_b = lax.ppermute(next_b, "ch", up)
    chain_a = lax.ppermute((chain_a.astype(F32) + next_a.astype(F32)).astype(BF16), "ch", up)
    chain_b = lax.ppermute((chain_b.astype(F32) + prev_b.astype(F32)).astype(BF16), "ch", down)

    payload = make_payload(observed, flags, pairs).reshape(64, 32, LANES)
    payload = lax.all_to_all(payload, "bl", split_axis=0, concat_axis=0, tiled=True)
    mine = lax.dynamic_slice(solver_order, (8 * lax.axis_index("bl"),), (8,))
    own_row = jnp.concatenate([mine, mine, jnp.full((LANES - 16,), -1, jnp.int32)]).astype(F32).reshape(1, LANES)
    order_row = solver_order.astype(F32).reshape(1, S)
    ohq, ohp, opt, vis_re, vis_im, kept = make_setup(payload.reshape(ROWS, LANES), order_row, own_row)

    model = pl.pallas_call(
        add_kernel, out_shape=jax.ShapeDtypeStruct((ROWS, 256), BF16), name="add"
    )(own_a, own_b, chain_a, chain_b, direct_a, direct_b)
    model = lax.all_to_all(model.reshape(64, 32, 256), "bl", split_axis=0, concat_axis=0, tiled=True)
    common = (model.reshape(ROWS, 256), opt, vis_re, vis_im, kept)

    for step in range(ITERS):
        if step == 0:
            mid = iterate(common, True)
        else:
            mid = iterate(common + (ohq, ohp, everyone.reshape(S, 256), gains), False)
        low = lax.ppermute(mid, "ch", up)
        high = lax.ppermute(mid, "ch", down)
        if step + 1 < ITERS:
            gains, block = smooth(where, mid, low, high, True)
            everyone = lax.all_to_all(block, "bl", split_axis=0, concat_axis=0, tiled=True)
        else:
            (gains,) = smooth(where, mid, low, high, False)
    return gains.reshape(8, 2, ND, 16).transpose(3, 2, 1, 0).reshape(16, 2 * ND, 8)


def solution(mesh):
    in_specs = (
        P(None, None, None, "ch"),
        P("bl", "ch"),
        P("bl"),
        P("ch", None, "bl"),
        P("ch", "bl"),
        P(None, "bl"),
        P(),
    )
    out_specs = P("ch", None, "bl")
    return jax.shard_map(body, mesh=mesh, in_specs=in_specs, out_specs=out_specs, check_vma=False)
```

```python
import jax
import jax.numpy as jnp
from jax import lax
from jax.experimental import pallas as pl
from jax.experimental.pallas import tpu as pltpu
from jax.sharding import Mesh, PartitionSpec as P

S = 512
ND = 8
ITERS = 4
LANES = 128
ROWS = 2048
HALF = 512
CHUNK = 256
F32 = jnp.float32
BF16 = jnp.bfloat16
BL = ("y", "z", "core")
SMALL = pltpu.CompilerParams(vmem_limit_bytes=16 << 20)


def nt(a, b):
    return lax.dot_general(a, b, (((1,), (1,)), ((), ())), preferred_element_type=F32)


def nn(a, b):
    return lax.dot_general(a, b, (((1,), (0,)), ((), ())), preferred_element_type=F32)


def iota(shape, dim):
    return lax.broadcasted_iota(jnp.int32, shape, dim)


def lane_order():
    lane = iota((256, 256), 0)
    source = (lane & 15) * 16 + ((lane >> 4) & 7) * 2 + (lane >> 7)
    return (iota((256, 256), 1) == source).astype(F32).astype(BF16)


def in_hbm(x):
    return pltpu.with_memory_space_constraint(x, pltpu.HBM)


def full(shape):
    return pl.BlockSpec(shape, lambda i, *scalars: (0,) * len(shape))


def degrid_kernel(count):
    def run(where_ref, tile_ref, kern_ref, *refs):
        facets, outs, tables = refs[:count], refs[count : 3 * count], refs[3 * count : 4 * count]
        order = lane_order()
        for index in range(count):
            for tile in range(4):
                tables[index][tile] = nn(order, facets[index][tile].reshape(256, 256)).astype(BF16)
        for block in range(4):
            rows = kern_ref[block * 16 : (block + 1) * 16].reshape(256, 256)
            place = slice((block % 2) * 256, (block % 2) * 256 + 256)
            for index in range(count):
                outs[2 * index + block // 2][place, :] = nt(rows, tables[index][tile_ref[block]]).astype(BF16)

    return run


def degrid(where, tile_of, kernel, facet_grid, groups):
    count = len(groups)

    def facet_spec(shift):
        return pl.BlockSpec((4, 16, 16, 256), lambda i, where, tile: (0, (where[0] + shift) & 3, 0, 0))

    half = jax.ShapeDtypeStruct((HALF, 256), BF16)
    table = pltpu.HBM((4, 256, 256), BF16)
    return pl.pallas_call(
        degrid_kernel(count),
        out_shape=[half] * (2 * count) + [table] * count,
        grid_spec=pltpu.PrefetchScalarGridSpec(
            num_scalar_prefetch=2,
            grid=(1,),
            in_specs=[full((64, 16, 256))] + [facet_spec(g) for g in groups],
            out_specs=[full((HALF, 256))] * (2 * count) + [full((4, 256, 256))] * count,
        ),
        compiler_params=SMALL,
    )(where, tile_of, in_hbm(kernel), *([in_hbm(facet_grid)] * count))


def late_kernel(jobs):
    def run(pay_ref, *refs):
        tables, outs = refs[:3], refs[3:]
        weight = (iota((LANES, 256), 0) == 52).astype(F32).astype(BF16)
        for half in range(2):

            def step(block, carry, half=half):
                segments = pl.ds(half * 32 + block * 16, 16)
                rows = pay_ref[segments, :16, :].reshape(256, 256)
                small = pay_ref[segments, 16:24, 128:].astype(F32).reshape(128, LANES)
                early = nn(small.astype(BF16), weight).reshape(16, 8, 256)
                late = nn(pltpu.roll(small, 64, 1).astype(BF16), weight).reshape(16, 8, 256)
                tile = jnp.concatenate([early, late], axis=1).reshape(256, 256)
                masked = [rows * (tile == float(t)).astype(F32).astype(BF16) for t in range(4)]
                place = pl.ds(pl.multiple_of(block * 256, 256), 256)
                for index, out in jobs[half]:
                    total = nt(masked[0], tables[index][0])
                    for t in range(1, 4):
                        total = total + nt(masked[t], tables[index][t])
                    outs[out][place, :] = total.astype(BF16)
                return carry

            lax.fori_loop(0, 2, step, 0, unroll=2)

    return run


def late_degrid(payload, tables, jobs, last):
    return pl.pallas_call(
        late_kernel(jobs),
        out_shape=[jax.ShapeDtypeStruct((HALF, 256), BF16)] * 2 + [last] * 2,
        compiler_params=SMALL,
        name="late",
    )(payload, *[in_hbm(table) for table in tables])


def payload_kernel(tile_ref, obs_ref, flag_ref, pair_ref, kern_ref, out_ref, kept_ref, stacked_ref):
    out_ref[:, :16, :] = kern_ref[...]
    kept = (1 - flag_ref[...]).astype(F32)
    pair = pair_ref[...]
    high = (pair >> 3).astype(F32)
    low = (pair & 7).astype(F32)
    block = iota((1, ROWS), 1) >> 9
    tile = jnp.where(block < 2, jnp.where(block == 0, tile_ref[0], tile_ref[1]), jnp.where(block == 2, tile_ref[2], tile_ref[3]))
    fill = jnp.zeros((LANES - 53, ROWS), F32)
    obs = obs_ref[...].astype(F32)
    stacked_ref[...] = jnp.concatenate([obs[:, 0], obs[:, 1], kept, high, low, tile.astype(F32), fill], axis=0)
    source = iota((LANES, 256), 0)
    col = iota((LANES, 256), 1)
    pick = (source == 32 + (col & 15)) & ((col < 32) | (col >= 128))
    pick = pick.astype(F32).astype(BF16)
    rest = (iota((LANES, LANES), 1) >= 32).astype(F32)

    def step(part, carry):
        turned = stacked_ref[:, pl.ds(pl.multiple_of(part * 128, 128), 128)].T
        wide = nn(turned.astype(BF16), pick)
        value = turned * (wide[:, :128] + rest)
        moved = pltpu.roll(value, 64, 1).reshape(4, 4, 8, LANES)
        value = value.reshape(4, 4, 8, LANES)
        segments = pl.ds(part * 4, 4)
        out_ref[segments, 16:24, :128] = (value[:, 0] + moved[:, 1]).astype(BF16)
        out_ref[segments, 16:24, 128:] = (value[:, 2] + moved[:, 3]).astype(BF16)
        kept = wide[:, 128:].reshape(4, 32, LANES)[:, :16].reshape(64, LANES).astype(BF16)
        kept_ref[pl.ds(pl.multiple_of(part * 64, 64), 64), :] = kept
        return carry

    lax.fori_loop(0, ROWS // 128, step, 0, unroll=4)


def make_payload(tile_of, observed, flags, pairs, kernel):
    return pl.pallas_call(
        payload_kernel,
        out_shape=[jax.ShapeDtypeStruct((64, 24, 256), BF16), jax.ShapeDtypeStruct((1024, LANES), BF16)],
        grid_spec=pltpu.PrefetchScalarGridSpec(
            num_scalar_prefetch=1,
            grid=(1,),
            in_specs=[
                full((16, 2, ROWS)),
                full((16, ROWS)),
                full((2, ROWS)),
                pl.BlockSpec((64, 16, 256), lambda i, tile: (0, 1, 0)),
            ],
            out_specs=[full((64, 24, 256)), full((1024, LANES))],
            scratch_shapes=[pltpu.VMEM((LANES, ROWS), F32)],
        ),
        compiler_params=SMALL,
        name="payload",
    )(tile_of, in_hbm(observed), in_hbm(flags), in_hbm(pairs), in_hbm(kernel))


def setup_kernel(pay_ref, order_ref, own_ref, ohq_ref, ohp_ref, opt_ref, vre_ref, vim_ref, kept_ref):
    source = iota((LANES, 5 * LANES), 0)
    col = iota((LANES, 5 * LANES), 1)
    piece = col >> 7
    weight = ((source == 16 * piece + (col & 15)) & (piece < 2)).astype(F32)
    weight = weight + 8.0 * ((source == 49) & (piece == 2)).astype(F32) + ((source == 51) & (piece == 2)).astype(F32)
    weight = weight + 8.0 * ((source == 48) & (piece == 3)).astype(F32) + ((source == 50) & (piece == 3)).astype(F32)
    weight = weight + ((source == 32 + (col & 15)) & (piece == 4)).astype(F32)
    weight = weight.astype(BF16)
    order = order_ref[...]
    own = own_ref[...]

    def step(i, carry):
        value = pay_ref[pl.ds(pl.multiple_of(i * 8, 8), 8), 16:24, :].astype(F32).reshape(64, 256)
        left, right = value[:, :128], value[:, 128:]
        value = jnp.concatenate([left, pltpu.roll(left, 64, 1), right, pltpu.roll(right, 64, 1)], axis=0)
        wide = nn(value.astype(BF16), weight).reshape(4, 8, 8, 5 * LANES)
        for part in range(2):
            rows = pl.ds(pl.multiple_of(i * 128 + part * 1024, 128), 128)
            mine = jnp.concatenate([wide[2 * part], wide[2 * part + 1]], axis=1).reshape(128, 5 * LANES)
            vre_ref[rows, :] = mine[:, :128].astype(BF16)
            vim_ref[rows, :] = mine[:, 128:256].astype(BF16)
            second = mine[:, 256:384]
            for quarter in range(4):
                lanes = slice(quarter * 128, (quarter + 1) * 128)
                ohq_ref[rows, lanes] = (second == order[:, lanes]).astype(F32).astype(BF16)
            near = (mine[:, 384:512] == own).astype(F32)
            ohp_ref[rows, :] = near.astype(BF16)
            opt_ref[:, rows] = near.T[:16, :].astype(BF16)
            if part == 1:
                kept_ref[pl.ds(pl.multiple_of(i * 128, 128), 128), :] = mine[:, 512:].astype(BF16)
        return carry

    lax.fori_loop(0, 8, step, 0)


def make_setup(payload, order, own):
    shapes = [
        jax.ShapeDtypeStruct((ROWS, S), BF16),
        jax.ShapeDtypeStruct((ROWS, LANES), BF16),
        jax.ShapeDtypeStruct((16, ROWS), BF16),
        pltpu.HBM((ROWS, LANES), BF16),
        pltpu.HBM((ROWS, LANES), BF16),
        pltpu.HBM((1024, LANES), BF16),
    ]
    return pl.pallas_call(setup_kernel, out_shape=shapes, compiler_params=SMALL, name="setup")(payload, order, own)


def over_directions(x):
    x = x + pltpu.roll(x, 16, 1)
    x = x + pltpu.roll(x, 32, 1)
    return x + pltpu.roll(x, 64, 1)


def iterate_kernel(first):
    def run(*refs):
        if first:
            model_a, *parts, opt_ref, vre_ref, vim_ref, out_ref, model_b, terms_ref = refs
            add_kernel(*parts, model_b)
        else:
            model_a, model_b, opt_ref, vre_ref, vim_ref, ohq_ref, ohp_ref, all_ref, own_ref, out_ref, terms_ref = refs
            all_gains = all_ref[...]
            own = own_ref[...]
            high = own.astype(BF16).astype(F32)
            near_gains = jnp.concatenate([high, own - high, jnp.zeros((LANES - 16, 256), F32)], axis=0).astype(BF16)

        for i in range(ROWS // CHUNK):
            rows = slice(i * CHUNK, (i + 1) * CHUNK)
            model = (model_a if i < 4 else model_b)[(i % 4) * CHUNK : (i % 4 + 1) * CHUNK, :].astype(F32)
            model_re, model_im = model[:, :128], model[:, 128:]
            if first:
                prod_re = pred_re = model_re
                prod_im = pred_im = model_im
            else:
                far = nn(ohq_ref[rows, :], all_gains)
                near = nn(ohp_ref[rows, :], near_gains)
                far_re, far_im = far[:, :128], far[:, 128:]
                near_re, near_im = near[:, :128], near[:, 128:]
                prod_re = model_re * far_re + model_im * far_im
                prod_im = model_im * far_re - model_re * far_im
                pred_re = near_re * prod_re - near_im * prod_im
                pred_im = near_re * prod_im + near_im * prod_re
            res_re = vre_ref[rows, :].astype(F32) - over_directions(pred_re)
            res_im = vim_ref[rows, :].astype(F32) - over_directions(pred_im)
            terms = jnp.concatenate(
                [
                    prod_re * res_re + prod_im * res_im,
                    prod_re * res_im - prod_im * res_re,
                    prod_re * prod_re + prod_im * prod_im,
                ],
                axis=1,
            )
            top = terms.astype(BF16)
            terms_ref[rows, :384] = top
            terms_ref[rows, 384:] = (terms - top.astype(F32)).astype(BF16)

        acc = nn(opt_ref[...], terms_ref[...])[:8]
        acc = acc[:, :384] + acc[:, 384:]
        sum_re, sum_im, power = acc[:, :128], acc[:, 128:256], acc[:, 256:]
        if first:
            gain_re = jnp.ones((8, 128), F32)
            gain_im = jnp.zeros((8, 128), F32)
        else:
            gain_re, gain_im = own[:, :128], own[:, 128:]
        new_re = (sum_re + gain_re * power) / (power + 1.0)
        new_im = (sum_im + gain_im * power) / (power + 1.0)
        out_ref[:, :128] = (gain_re + new_re) * 0.5
        out_ref[:, 128:] = (gain_im + new_im) * 0.5

    return run


def iterate(args, first):
    return pl.pallas_call(
        iterate_kernel(first),
        out_shape=[jax.ShapeDtypeStruct((8, 256), F32)] + [jax.ShapeDtypeStruct((1024, 256), BF16)] * first,
        scratch_shapes=[pltpu.VMEM((ROWS, 768), BF16)],
        compiler_params=SMALL,
        name="iterate0" if first else "iterate",
    )(*args)


def smooth_kernel(spread):
    def run(where_ref, mid_ref, low_ref, high_ref, out_ref, *more):
        chan = iota((8, LANES), 1) & 15
        whole = chan + 16 * where_ref[0]
        has_left = (whole > 0).astype(F32)
        has_right = (whole < 63).astype(F32)
        for part in range(2):
            lanes = slice(part * 128, (part + 1) * 128)
            mid = mid_ref[:, lanes]
            left = jnp.where(chan == 0, pltpu.roll(low_ref[:, lanes], 113, 1), pltpu.roll(mid, 1, 1))
            right = jnp.where(chan == 15, pltpu.roll(high_ref[:, lanes], 15, 1), pltpu.roll(mid, 127, 1))
            total = 0.25 * has_left * left + 0.5 * mid + 0.25 * has_right * right
            out_ref[:, lanes] = total / (0.5 + 0.25 * has_left + 0.25 * has_right)
        if spread:
            more[0][...] = jnp.broadcast_to(out_ref[...].astype(BF16)[None], (32, 8, 256))

    return run


def smooth(where, mid, low, high, spread):
    shapes = [jax.ShapeDtypeStruct((8, 256), F32)]
    if spread:
        shapes.append(jax.ShapeDtypeStruct((32, 8, 256), BF16))
    smem = pl.BlockSpec(memory_space=pltpu.SMEM)
    vmem = pl.BlockSpec(memory_space=pltpu.VMEM)
    return pl.pallas_call(
        smooth_kernel(spread),
        out_shape=shapes,
        in_specs=[smem, vmem, vmem, vmem],
        out_specs=[vmem] * len(shapes),
        compiler_params=SMALL,
        name="smooth",
    )(where, mid, low, high)


def pair_kernel(left_ref, right_ref, out_ref):
    for part in range(2):
        rows = slice(part * 256, (part + 1) * 256)
        out_ref[rows, :] = (left_ref[rows, :].astype(F32) + right_ref[rows, :].astype(F32)).astype(BF16)


def pair_sum(left, right):
    return pl.pallas_call(
        pair_kernel, out_shape=jax.ShapeDtypeStruct((HALF, 256), BF16), compiler_params=SMALL, name="pair"
    )(left, right)


def add_kernel(own_a, own_b, chain_a, chain_b, near_a, near_b, kept_ref, out_ref):
    for half, parts in ((0, (own_a, chain_a, near_a)), (1, (own_b, chain_b, near_b))):
        for part in range(2):
            near = slice(part * 256, (part + 1) * 256)
            rows = slice(half * HALF + part * 256, half * HALF + (part + 1) * 256)
            total = parts[0][near, :].astype(F32) + parts[1][near, :].astype(F32) + parts[2][near, :].astype(F32)
            kept = kept_ref[rows, :].astype(F32)
            out_ref[rows, :128] = (total[:, :128] * kept).astype(BF16)
            out_ref[rows, 128:] = (total[:, 128:] * kept).astype(BF16)


def total(*parts):
    return pl.pallas_call(
        add_kernel, out_shape=jax.ShapeDtypeStruct((1024, 256), BF16), compiler_params=SMALL, name="add"
    )(*parts)


UP = [(i, (i + 1) % 4) for i in range(4)]
DOWN = [(i, (i + 3) % 4) for i in range(4)]


def last_legs(chain_a, chain_b, direct_a, direct_b, next_a, prev_b):
    chain_a = lax.ppermute(pair_sum(chain_a, next_a), "ch", UP)
    chain_b = lax.ppermute(pair_sum(chain_b, prev_b), "ch", DOWN)
    return chain_a, chain_b, direct_a, direct_b


def exchange(value):
    return lax.all_to_all(value, BL, split_axis=0, concat_axis=0, tiled=True)


def body(facet_grid, kernel, tile_of, observed, flags, pairs, solver_order):
    where = lax.axis_index("ch").astype(jnp.int32).reshape(1)
    kernel = kernel.reshape(64, 32, 256)
    payload, kept_a = make_payload(tile_of, observed, flags, pairs, kernel)
    arrived = exchange(payload)

    mine = lax.dynamic_slice(solver_order, (8 * lax.axis_index(BL),), (8,))
    own_row = jnp.concatenate([mine, mine, jnp.full((LANES - 16,), -1, jnp.int32)]).astype(F32).reshape(1, LANES)
    order_row = solver_order.reshape(32, 2, 8).transpose(1, 0, 2).astype(F32).reshape(1, S)

    far_a, far_b, table2 = degrid(where, tile_of, kernel, facet_grid, (2,))
    chain_a = lax.ppermute(far_a, "ch", UP)
    chain_b = lax.ppermute(far_b, "ch", DOWN)
    next_a, next_b, prev_a, prev_b, own_a, own_b, table1, table3, table0 = degrid(
        where, tile_of, kernel, facet_grid, (1, 3, 0)
    )
    direct_a = lax.ppermute(prev_a, "ch", DOWN)
    direct_b = lax.ppermute(next_b, "ch", UP)
    legs = last_legs(chain_a, chain_b, direct_a, direct_b, next_a, prev_b)
    model_a = total(own_a, own_b, *legs, kept_a)

    near = jax.ShapeDtypeStruct((HALF, 256), BF16)
    away = pltpu.HBM((HALF, 256), BF16)
    far_a, far_b, prev_a, next_b = late_degrid(
        arrived, (table2, table3, table1), (((0, 0), (1, 2)), ((0, 1), (2, 3))), near
    )
    chain_a = lax.ppermute(far_a, "ch", UP)
    chain_b = lax.ppermute(far_b, "ch", DOWN)
    direct_a = lax.ppermute(prev_a, "ch", DOWN)
    direct_b = lax.ppermute(next_b, "ch", UP)
    next_a, prev_b, own_a, own_b = late_degrid(
        arrived, (table1, table3, table0), (((0, 0), (2, 2)), ((1, 1), (2, 3))), away
    )
    ohq, ohp, opt, vis_re, vis_im, kept_b = make_setup(arrived, order_row, own_row)
    legs = last_legs(chain_a, chain_b, direct_a, direct_b, next_a, prev_b)
    model_a = exchange(model_a.reshape(64, 16, 256)).reshape(1024, 256)

    for step in range(ITERS):
        if step == 0:
            parts = (in_hbm(own_a), in_hbm(own_b), *legs, in_hbm(kept_b))
            mid, model_b = iterate((model_a, *parts, opt, in_hbm(vis_re), in_hbm(vis_im)), True)
        else:
            rows = (model_a, model_b, opt, vis_re, vis_im, ohq, ohp)
            (mid,) = iterate(rows + (everyone.reshape(S, 256), gains), False)
        low = lax.ppermute(mid, "ch", UP)
        high = lax.ppermute(mid, "ch", DOWN)
        if step + 1 < ITERS:
            gains, block = smooth(where, mid, low, high, True)
            everyone = lax.all_to_all(block, ("y", "z"), split_axis=0, concat_axis=0, tiled=True)
            everyone = lax.all_gather(everyone, "core", axis=0, tiled=True)
        else:
            (gains,) = smooth(where, mid, low, high, False)
    return gains.reshape(8, 2, ND, 16).transpose(3, 2, 1, 0).reshape(16, 2 * ND, 8)


def solution(mesh):
    split = Mesh(mesh.devices.reshape(4, 8, 2, 4), BL + ("ch",))
    in_specs = (
        P(None, None, None, "ch"),
        P(BL, "ch"),
        P(BL),
        P("ch", None, BL),
        P("ch", BL),
        P(None, BL),
        P(),
    )
    out_specs = P("ch", None, BL)
    return jax.shard_map(body, mesh=split, in_specs=in_specs, out_specs=out_specs, check_vma=False)
```

```python
import jax
import jax.numpy as jnp
from jax import lax
from jax.experimental import pallas as pl
from jax.experimental.pallas import tpu as pltpu
from jax.sharding import Mesh, PartitionSpec as P

S = 512
ND = 8
ITERS = 4
LANES = 128
ROWS = 2048
HALF = 512
CHUNK = 256
F32 = jnp.float32
BF16 = jnp.bfloat16
BL = ("y", "z", "core")
SMALL = pltpu.CompilerParams(vmem_limit_bytes=16 << 20)


def nt(a, b):
    return lax.dot_general(a, b, (((1,), (1,)), ((), ())), preferred_element_type=F32)


def nn(a, b):
    return lax.dot_general(a, b, (((1,), (0,)), ((), ())), preferred_element_type=F32)


def iota(shape, dim):
    return lax.broadcasted_iota(jnp.int32, shape, dim)


def lane_order():
    lane = iota((256, 256), 0)
    source = (lane & 15) * 16 + ((lane >> 4) & 7) * 2 + (lane >> 7)
    return (iota((256, 256), 1) == source).astype(F32).astype(BF16)


def in_hbm(x):
    return pltpu.with_memory_space_constraint(x, pltpu.HBM)


def full(shape):
    return pl.BlockSpec(shape, lambda i, *scalars: (0,) * len(shape))


def degrid_kernel(count):
    def run(where_ref, tile_ref, kern_ref, *refs):
        facets, outs, tables = refs[:count], refs[count : 3 * count], refs[3 * count : 4 * count]
        order = lane_order()
        for index in range(count):
            for tile in range(4):
                columns = slice(tile * 256, (tile + 1) * 256)
                tables[index][:, columns] = nn(order, facets[index][tile].reshape(256, 256)).astype(BF16)
        for block in range(4):
            rows = kern_ref[block * 16 : (block + 1) * 16].reshape(256, 256)
            place = slice((block % 2) * 256, (block % 2) * 256 + 256)
            columns = pl.ds(pl.multiple_of(tile_ref[block] * 256, 256), 256)
            for index in range(count):
                outs[2 * index + block // 2][place, :] = nt(rows, tables[index][:, columns]).astype(BF16)

    return run


def degrid(where, tile_of, kernel, facet_grid, groups):
    count = len(groups)

    def facet_spec(shift):
        return pl.BlockSpec((4, 16, 16, 256), lambda i, where, tile: (0, (where[0] + shift) & 3, 0, 0))

    half = jax.ShapeDtypeStruct((HALF, 256), BF16)
    table = pltpu.HBM((256, 1024), BF16)
    return pl.pallas_call(
        degrid_kernel(count),
        out_shape=[half] * (2 * count) + [table] * count,
        grid_spec=pltpu.PrefetchScalarGridSpec(
            num_scalar_prefetch=2,
            grid=(1,),
            in_specs=[full((64, 16, 256))] + [facet_spec(g) for g in groups],
            out_specs=[full((HALF, 256))] * (2 * count) + [full((256, 1024))] * count,
        ),
        compiler_params=SMALL,
    )(where, tile_of, in_hbm(kernel), *([in_hbm(facet_grid)] * count))


def late_kernel(jobs):
    def run(pay_ref, first_ref, second_ref, third_ref, *refs):
        outs, (lhs_ref, table_ref, sems) = refs[:-3], refs[-3:]
        loads = [
            pltpu.make_async_copy(source, table_ref.at[index], sems.at[index])
            for index, source in enumerate((first_ref, second_ref, third_ref))
        ]
        for load in loads:
            load.start()
        weight = (iota((LANES, 256), 0) == 52).astype(F32).astype(BF16)

        def mask(block, carry):
            segments = pl.ds(block * 16, 16)
            rows = pay_ref[segments, :16, :].reshape(256, 256)
            small = pay_ref[segments, 16:24, 128:].astype(F32).reshape(128, LANES)
            early = nn(small.astype(BF16), weight).reshape(16, 8, 256)
            late = nn(pltpu.roll(small, 64, 1).astype(BF16), weight).reshape(16, 8, 256)
            tile = jnp.concatenate([early, late], axis=1).reshape(256, 256)
            place = pl.ds(pl.multiple_of(block * 256, 256), 256)
            for t in range(4):
                lhs_ref[place, t * 256 : (t + 1) * 256] = rows * (tile == float(t)).astype(F32).astype(BF16)
            return carry

        lax.fori_loop(0, 4, mask, 0, unroll=2)
        for load in loads:
            load.wait()
        for half in range(2):
            for index, out, start in jobs[half]:

                def step(block, carry, half=half, index=index, out=out, start=start):
                    source = pl.ds(pl.multiple_of(half * 512 + block * 256, 256), 256)
                    place = pl.ds(pl.multiple_of(start + block * 256, 256), 256)
                    outs[out][place, :] = nt(lhs_ref[source, :], table_ref[index]).astype(BF16)
                    return carry

                lax.fori_loop(0, 2, step, 0, unroll=2)

    return run


def late_degrid(payload, tables, jobs, shapes):
    vmem = pl.BlockSpec(memory_space=pltpu.VMEM)
    anywhere = pl.BlockSpec(memory_space=pl.ANY)
    return pl.pallas_call(
        late_kernel(jobs),
        out_shape=shapes,
        in_specs=[vmem, anywhere, anywhere, anywhere],
        out_specs=[vmem] * len(shapes),
        scratch_shapes=[
            pltpu.VMEM((1024, 1024), BF16),
            pltpu.VMEM((3, 256, 1024), BF16),
            pltpu.SemaphoreType.DMA((3,)),
        ],
        compiler_params=SMALL,
        name="late",
    )(payload, *[in_hbm(table) for table in tables])


def payload_kernel(tile_ref, obs_ref, flag_ref, pair_ref, kern_ref, out_ref, kept_ref, stacked_ref, sem):
    bulk = pltpu.make_async_copy(kern_ref.at[:, 16:32, :], out_ref.at[:, 0:16, :], sem)
    bulk.start()
    kept = (1 - flag_ref[...]).astype(F32)
    pair = pair_ref[...]
    high = (pair >> 3).astype(F32)
    low = (pair & 7).astype(F32)
    block = iota((1, ROWS), 1) >> 9
    tile = jnp.where(block < 2, jnp.where(block == 0, tile_ref[0], tile_ref[1]), jnp.where(block == 2, tile_ref[2], tile_ref[3]))
    fill = jnp.zeros((LANES - 53, ROWS), F32)
    obs = obs_ref[...].astype(F32)
    stacked_ref[...] = jnp.concatenate([obs[:, 0], obs[:, 1], kept, high, low, tile.astype(F32), fill], axis=0)
    source = iota((LANES, 256), 0)
    col = iota((LANES, 256), 1)
    pick = (source == 32 + (col & 15)) & ((col < 32) | (col >= 128))
    pick = pick.astype(F32).astype(BF16)
    rest = (iota((LANES, LANES), 1) >= 32).astype(F32)

    def step(part, carry):
        turned = stacked_ref[:, pl.ds(pl.multiple_of(part * 128, 128), 128)].T
        wide = nn(turned.astype(BF16), pick)
        value = turned * (wide[:, :128] + rest)
        moved = pltpu.roll(value, 64, 1).reshape(4, 4, 8, LANES)
        value = value.reshape(4, 4, 8, LANES)
        segments = pl.ds(part * 4, 4)
        out_ref[segments, 16:24, :128] = (value[:, 0] + moved[:, 1]).astype(BF16)
        out_ref[segments, 16:24, 128:] = (value[:, 2] + moved[:, 3]).astype(BF16)
        kept = wide[:, 128:].reshape(4, 32, LANES)[:, :16].reshape(64, LANES).astype(BF16)
        kept_ref[pl.ds(pl.multiple_of(part * 64, 64), 64), :] = kept
        return carry

    lax.fori_loop(0, ROWS // 128, step, 0, unroll=4)
    bulk.wait()


def make_payload(tile_of, observed, flags, pairs, kernel):
    return pl.pallas_call(
        payload_kernel,
        out_shape=[jax.ShapeDtypeStruct((64, 24, 256), BF16), jax.ShapeDtypeStruct((1024, LANES), BF16)],
        grid_spec=pltpu.PrefetchScalarGridSpec(
            num_scalar_prefetch=1,
            grid=(1,),
            in_specs=[
                full((16, 2, ROWS)),
                full((16, ROWS)),
                full((2, ROWS)),
                pl.BlockSpec(memory_space=pl.ANY),
            ],
            out_specs=[full((64, 24, 256)), full((1024, LANES))],
            scratch_shapes=[pltpu.VMEM((LANES, ROWS), F32), pltpu.SemaphoreType.DMA],
        ),
        compiler_params=SMALL,
        name="payload",
    )(tile_of, in_hbm(observed), in_hbm(flags), in_hbm(pairs), in_hbm(kernel))


def setup_kernel(pay_ref, order_ref, own_ref, ohq_ref, ohp_ref, opt_ref, vre_ref, vim_ref, kept_ref):
    source = iota((LANES, 5 * LANES), 0)
    col = iota((LANES, 5 * LANES), 1)
    piece = col >> 7
    weight = ((source == 16 * piece + (col & 15)) & (piece < 2)).astype(F32)
    weight = weight + 8.0 * ((source == 49) & (piece == 2)).astype(F32) + ((source == 51) & (piece == 2)).astype(F32)
    weight = weight + 8.0 * ((source == 48) & (piece == 3)).astype(F32) + ((source == 50) & (piece == 3)).astype(F32)
    weight = weight + ((source == 32 + (col & 15)) & (piece == 4)).astype(F32)
    weight = weight.astype(BF16)
    order = order_ref[...]
    own = own_ref[...]

    def step(i, carry):
        value = pay_ref[pl.ds(pl.multiple_of(i * 8, 8), 8), 16:24, :].astype(F32).reshape(64, 256)
        left, right = value[:, :128], value[:, 128:]
        value = jnp.concatenate([left, pltpu.roll(left, 64, 1), right, pltpu.roll(right, 64, 1)], axis=0)
        wide = nn(value.astype(BF16), weight).reshape(4, 8, 8, 5 * LANES)
        for part in range(2):
            rows = pl.ds(pl.multiple_of(i * 128 + part * 1024, 128), 128)
            mine = jnp.concatenate([wide[2 * part], wide[2 * part + 1]], axis=1).reshape(128, 5 * LANES)
            vre_ref[rows, :] = mine[:, :128].astype(BF16)
            vim_ref[rows, :] = mine[:, 128:256].astype(BF16)
            second = mine[:, 256:384]
            for quarter in range(4):
                lanes = slice(quarter * 128, (quarter + 1) * 128)
                ohq_ref[rows, lanes] = (second == order[:, lanes]).astype(F32).astype(BF16)
            near = (mine[:, 384:512] == own).astype(F32)
            ohp_ref[rows, :] = near.astype(BF16)
            opt_ref[:, rows] = near.T[:16, :].astype(BF16)
            if part == 1:
                kept_ref[pl.ds(pl.multiple_of(i * 128, 128), 128), :] = mine[:, 512:].astype(BF16)
        return carry

    lax.fori_loop(0, 8, step, 0)


def make_setup(payload, order, own):
    shapes = [
        pltpu.HBM((ROWS, S), BF16),
        pltpu.HBM((ROWS, LANES), BF16),
        jax.ShapeDtypeStruct((16, ROWS), BF16),
        pltpu.HBM((ROWS, LANES), BF16),
        pltpu.HBM((ROWS, LANES), BF16),
        pltpu.HBM((1024, LANES), BF16),
    ]
    return pl.pallas_call(setup_kernel, out_shape=shapes, compiler_params=SMALL, name="setup")(payload, order, own)


def over_directions(x):
    x = x + pltpu.roll(x, 16, 1)
    x = x + pltpu.roll(x, 32, 1)
    return x + pltpu.roll(x, 64, 1)


def iterate_kernel(first):
    def run(*refs):
        if first:
            model_a, chain_a, chain_b, opt_ref, *sources = refs[:11]
            out_ref, model_b, terms_ref, vre_ref, vim_ref, kept_ref, own_a, own_b, near_a, near_b, sems = refs[11:]
            vre_source, vim_source, kept_source, a_source, b_source, low_source, high_source = sources
            early, late = slice(0, 1024), slice(1024, 2048)
            moves = [
                (vre_source.at[early], vre_ref.at[early]),
                (vim_source.at[early], vim_ref.at[early]),
                (kept_source, kept_ref),
                (a_source, own_a),
                (b_source, own_b),
                (high_source.at[HALF:], near_a),
                (low_source.at[HALF:], near_b),
                (vre_source.at[late], vre_ref.at[late]),
                (vim_source.at[late], vim_ref.at[late]),
            ]
            moves = [pltpu.make_async_copy(*move, sems.at[index]) for index, move in enumerate(moves)]
            for move in moves:
                move.start()
        else:
            model_a, model_b, opt_ref, vre_ref, vim_ref, ohq_ref, ohp_ref, here_ref, there_ref, own_ref, out_ref, terms_ref = refs
            all_gains = jnp.concatenate([here_ref[...], there_ref[...]], axis=0)
            own = own_ref[...]
            high = own.astype(BF16).astype(F32)
            near_gains = jnp.concatenate([high, own - high, jnp.zeros((LANES - 16, 256), F32)], axis=0).astype(BF16)

        for i in range(ROWS // CHUNK):
            if first and i == 0:
                moves[0].wait()
                moves[1].wait()
            if first and i == 4:
                for move in moves[2:]:
                    move.wait()
                add_kernel(own_a, own_b, chain_a, chain_b, near_a, near_b, kept_ref, model_b)
            rows = slice(i * CHUNK, (i + 1) * CHUNK)
            model = (model_a if i < 4 else model_b)[(i % 4) * CHUNK : (i % 4 + 1) * CHUNK, :].astype(F32)
            model_re, model_im = model[:, :128], model[:, 128:]
            if first:
                prod_re = pred_re = model_re
                prod_im = pred_im = model_im
            else:
                far = nn(ohq_ref[rows, :], all_gains)
                near = nn(ohp_ref[rows, :], near_gains)
                far_re, far_im = far[:, :128], far[:, 128:]
                near_re, near_im = near[:, :128], near[:, 128:]
                prod_re = model_re * far_re + model_im * far_im
                prod_im = model_im * far_re - model_re * far_im
                pred_re = near_re * prod_re - near_im * prod_im
                pred_im = near_re * prod_im + near_im * prod_re
            res_re = vre_ref[rows, :].astype(F32) - over_directions(pred_re)
            res_im = vim_ref[rows, :].astype(F32) - over_directions(pred_im)
            terms = jnp.concatenate(
                [
                    prod_re * res_re + prod_im * res_im,
                    prod_re * res_im - prod_im * res_re,
                    prod_re * prod_re + prod_im * prod_im,
                ],
                axis=1,
            )
            top = terms.astype(BF16)
            terms_ref[rows, :384] = top
            terms_ref[rows, 384:] = (terms - top.astype(F32)).astype(BF16)

        acc = nn(opt_ref[...], terms_ref[...])[:8]
        acc = acc[:, :384] + acc[:, 384:]
        sum_re, sum_im, power = acc[:, :128], acc[:, 128:256], acc[:, 256:]
        if first:
            gain_re = jnp.ones((8, 128), F32)
            gain_im = jnp.zeros((8, 128), F32)
        else:
            gain_re, gain_im = own[:, :128], own[:, 128:]
        new_re = (sum_re + gain_re * power) / (power + 1.0)
        new_im = (sum_im + gain_im * power) / (power + 1.0)
        out_ref[:, :128] = (gain_re + new_re) * 0.5
        out_ref[:, 128:] = (gain_im + new_im) * 0.5

    return run


def iterate(args, first):
    vmem = pl.BlockSpec(memory_space=pltpu.VMEM)
    anywhere = pl.BlockSpec(memory_space=pl.ANY)
    scratch = [pltpu.VMEM((ROWS, 768), BF16)]
    if first:
        scratch += [pltpu.VMEM((ROWS, LANES), BF16)] * 2 + [pltpu.VMEM((1024, LANES), BF16)]
        scratch += [pltpu.VMEM((HALF, 256), BF16)] * 4 + [pltpu.SemaphoreType.DMA((9,))]
    return pl.pallas_call(
        iterate_kernel(first),
        out_shape=[jax.ShapeDtypeStruct((8, 256), F32)] + [jax.ShapeDtypeStruct((1024, 256), BF16)] * first,
        in_specs=[vmem] * 4 + [anywhere] * 7 if first else [vmem] * len(args),
        out_specs=[vmem] * (2 if first else 1),
        scratch_shapes=scratch,
        compiler_params=SMALL,
        name="iterate0" if first else "iterate",
    )(*args)


def smooth_kernel(spread):
    def run(where_ref, mid_ref, low_ref, high_ref, out_ref, *more):
        chan = iota((8, LANES), 1) & 15
        whole = chan + 16 * where_ref[0]
        has_left = (whole > 0).astype(F32)
        has_right = (whole < 63).astype(F32)
        for part in range(2):
            lanes = slice(part * 128, (part + 1) * 128)
            mid = mid_ref[:, lanes]
            left = jnp.where(chan == 0, pltpu.roll(low_ref[:, lanes], 113, 1), pltpu.roll(mid, 1, 1))
            right = jnp.where(chan == 15, pltpu.roll(high_ref[:, lanes], 15, 1), pltpu.roll(mid, 127, 1))
            total = 0.25 * has_left * left + 0.5 * mid + 0.25 * has_right * right
            out_ref[:, lanes] = total / (0.5 + 0.25 * has_left + 0.25 * has_right)
        if spread:
            more[0][...] = jnp.broadcast_to(out_ref[...].astype(BF16)[None], (32, 8, 256))

    return run


def smooth(where, mid, low, high, spread):
    shapes = [jax.ShapeDtypeStruct((8, 256), F32)]
    if spread:
        shapes.append(jax.ShapeDtypeStruct((32, 8, 256), BF16))
    smem = pl.BlockSpec(memory_space=pltpu.SMEM)
    vmem = pl.BlockSpec(memory_space=pltpu.VMEM)
    return pl.pallas_call(
        smooth_kernel(spread),
        out_shape=shapes,
        in_specs=[smem, vmem, vmem, vmem],
        out_specs=[vmem] * len(shapes),
        compiler_params=SMALL,
        name="smooth",
    )(where, mid, low, high)


def pair_kernel(left_ref, right_ref, out_ref):
    for part in range(2):
        rows = slice(part * 256, (part + 1) * 256)
        out_ref[rows, :] = (left_ref[rows, :].astype(F32) + right_ref[rows, :].astype(F32)).astype(BF16)


def pair_sum(left, right):
    block = pl.BlockSpec((HALF, 256), lambda i: (0, 0))
    return pl.pallas_call(
        pair_kernel,
        out_shape=jax.ShapeDtypeStruct((HALF, 256), BF16),
        grid=(1,),
        in_specs=[block, block],
        out_specs=block,
        compiler_params=SMALL,
        name="pair",
    )(in_hbm(left) if left.shape[0] > HALF else left, right)


def add_kernel(own_a, own_b, chain_a, chain_b, near_a, near_b, kept_ref, out_ref):
    for half, parts in ((0, (own_a, chain_a, near_a)), (1, (own_b, chain_b, near_b))):
        for part in range(2):
            near = slice(part * 256, (part + 1) * 256)
            rows = slice(half * HALF + part * 256, half * HALF + (part + 1) * 256)
            total = parts[0][near, :].astype(F32) + parts[1][near, :].astype(F32) + parts[2][near, :].astype(F32)
            kept = kept_ref[rows, :].astype(F32)
            out_ref[rows, :128] = (total[:, :128] * kept).astype(BF16)
            out_ref[rows, 128:] = (total[:, 128:] * kept).astype(BF16)


def total(*parts):
    return pl.pallas_call(
        add_kernel, out_shape=jax.ShapeDtypeStruct((1024, 256), BF16), compiler_params=SMALL, name="add"
    )(*parts)


UP = [(i, (i + 1) % 4) for i in range(4)]
DOWN = [(i, (i + 3) % 4) for i in range(4)]


def last_legs(chain_a, chain_b, direct_a, direct_b, next_a, prev_b):
    chain_a = lax.ppermute(pair_sum(chain_a, next_a), "ch", UP)
    chain_b = lax.ppermute(pair_sum(chain_b, prev_b), "ch", DOWN)
    return chain_a, chain_b, direct_a, direct_b


def exchange(value):
    return lax.all_to_all(value, BL, split_axis=0, concat_axis=0, tiled=True)


def body(facet_grid, kernel, tile_of, observed, flags, pairs, solver_order):
    where = lax.axis_index("ch").astype(jnp.int32).reshape(1)
    kernel = kernel.reshape(64, 32, 256)
    payload, kept_a = make_payload(tile_of, observed, flags, pairs, kernel)
    arrived = exchange(payload)

    mine = lax.dynamic_slice(solver_order, (8 * lax.axis_index(BL),), (8,))
    own_row = jnp.concatenate([mine, mine, jnp.full((LANES - 16,), -1, jnp.int32)]).astype(F32).reshape(1, LANES)
    halves = solver_order.reshape(32, 2, 8).transpose(1, 0, 2).astype(F32).reshape(2, S // 2)
    order_row = jnp.where(lax.axis_index("core") == 0, halves, halves[::-1]).reshape(1, S)

    far_a, far_b, table2 = degrid(where, tile_of, kernel, facet_grid, (2,))
    chain_a = lax.ppermute(far_a, "ch", UP)
    chain_b = lax.ppermute(far_b, "ch", DOWN)
    next_a, next_b, prev_a, prev_b, own_a, own_b, table1, table3, table0 = degrid(
        where, tile_of, kernel, facet_grid, (1, 3, 0)
    )
    direct_a = lax.ppermute(prev_a, "ch", DOWN)
    direct_b = lax.ppermute(next_b, "ch", UP)
    legs = last_legs(chain_a, chain_b, direct_a, direct_b, next_a, prev_b)
    model_a = total(own_a, own_b, *legs, kept_a)

    half = jax.ShapeDtypeStruct((HALF, 256), BF16)
    away = pltpu.HBM((HALF, 256), BF16)
    whole = pltpu.HBM((2 * HALF, 256), BF16)
    going_up, going_down = late_degrid(
        arrived,
        (table2, table3, table1),
        (((0, 0, 0), (1, 1, HALF)), ((0, 1, 0), (2, 0, HALF))),
        [whole, whole],
    )
    from_low = lax.ppermute(going_up, "ch", UP)
    from_high = lax.ppermute(going_down, "ch", DOWN)
    next_a, prev_b, own_a, own_b = late_degrid(
        arrived, (table1, table3, table0), (((0, 0, 0), (2, 2, 0)), ((1, 1, 0), (2, 3, 0))), [half, half, away, away]
    )
    ohq, ohp, opt, vis_re, vis_im, kept_b = make_setup(arrived, order_row, own_row)
    chain_a, chain_b, *_ = last_legs(from_low, from_high, None, None, next_a, prev_b)
    model_a = exchange(model_a.reshape(64, 16, 256)).reshape(1024, 256)

    for step in range(ITERS):
        if step == 0:
            sources = map(in_hbm, (vis_re, vis_im, kept_b, own_a, own_b, from_low, from_high))
            mid, model_b = iterate((model_a, chain_a, chain_b, opt, *sources), True)
        else:
            rows = (model_a, model_b, opt, vis_re, vis_im, ohq, ohp)
            both = (everyone.reshape(S // 2, 256), others.reshape(S // 2, 256))
            (mid,) = iterate(rows + both + (gains,), False)
        low = lax.ppermute(mid, "ch", UP)
        high = lax.ppermute(mid, "ch", DOWN)
        if step + 1 < ITERS:
            gains, block = smooth(where, mid, low, high, True)
            everyone = lax.all_to_all(block, ("y", "z"), split_axis=0, concat_axis=0, tiled=True)
            others = lax.ppermute(everyone, "core", [(0, 1), (1, 0)])
        else:
            (gains,) = smooth(where, mid, low, high, False)
    return gains.reshape(8, 2, ND, 16).transpose(3, 2, 1, 0).reshape(16, 2 * ND, 8)


def solution(mesh):
    split = Mesh(mesh.devices.reshape(4, 8, 2, 4), BL + ("ch",))
    in_specs = (
        P(None, None, None, "ch"),
        P(BL, "ch"),
        P(BL),
        P("ch", None, BL),
        P("ch", BL),
        P(None, BL),
        P(),
    )
    out_specs = P("ch", None, BL)
    return jax.shard_map(body, mesh=split, in_specs=in_specs, out_specs=out_specs, check_vma=False)
```

```python
import jax
import jax.numpy as jnp
from jax import lax
from jax.experimental import pallas as pl
from jax.experimental.pallas import tpu as pltpu
from jax.sharding import Mesh, PartitionSpec as P

S = 512
ITERS = 4
LANES = 128
ROWS = 2048
HALF = 512
CHUNK = 256
F32 = jnp.float32
BF16 = jnp.bfloat16
BL = ("y", "z", "core")
SMALL = pltpu.CompilerParams(vmem_limit_bytes=16 << 20)


def nt(a, b):
    return lax.dot_general(a, b, (((1,), (1,)), ((), ())), preferred_element_type=F32)


def nn(a, b):
    return lax.dot_general(a, b, (((1,), (0,)), ((), ())), preferred_element_type=F32)


def iota(shape, dim):
    return lax.broadcasted_iota(jnp.int32, shape, dim)


def lane_order():
    lane = iota((256, 256), 0)
    source = (lane & 15) * 16 + ((lane >> 4) & 7) * 2 + (lane >> 7)
    return (iota((256, 256), 1) == source).astype(F32).astype(BF16)


def in_hbm(x):
    return pltpu.with_memory_space_constraint(x, pltpu.HBM)


def full(shape):
    return pl.BlockSpec(shape, lambda i, *scalars: (0,) * len(shape))


def degrid_kernel(count):
    def run(where_ref, tile_ref, kern_ref, *refs):
        facets, outs, tables = refs[:count], refs[count : 3 * count], refs[3 * count : 4 * count]
        order = lane_order()
        for index in range(count):
            for tile in range(4):
                columns = slice(tile * 256, (tile + 1) * 256)
                tables[index][:, columns] = nn(order, facets[index][tile].reshape(256, 256)).astype(BF16)
        for block in range(4):
            rows = kern_ref[block * 16 : (block + 1) * 16].reshape(256, 256)
            place = slice((block % 2) * 256, (block % 2) * 256 + 256)
            columns = pl.ds(pl.multiple_of(tile_ref[block] * 256, 256), 256)
            for index in range(count):
                outs[2 * index + block // 2][place, :] = nt(rows, tables[index][:, columns]).astype(BF16)

    return run


def degrid(where, tile_of, kernel, facet_grid, groups):
    count = len(groups)

    def facet_spec(shift):
        return pl.BlockSpec((4, 16, 16, 256), lambda i, where, tile: (0, (where[0] + shift) & 3, 0, 0))

    half = jax.ShapeDtypeStruct((HALF, 256), BF16)
    table = pltpu.HBM((256, 1024), BF16)
    return pl.pallas_call(
        degrid_kernel(count),
        out_shape=[half] * (2 * count) + [table] * count,
        grid_spec=pltpu.PrefetchScalarGridSpec(
            num_scalar_prefetch=2,
            grid=(1,),
            in_specs=[full((64, 16, 256))] + [facet_spec(g) for g in groups],
            out_specs=[full((HALF, 256))] * (2 * count) + [full((256, 1024))] * count,
        ),
        compiler_params=SMALL,
    )(where, tile_of, in_hbm(kernel), *([in_hbm(facet_grid)] * count))


def late_kernel(jobs):
    def run(pay_ref, first_ref, second_ref, third_ref, *refs):
        outs, (lhs_ref, table_ref, sems) = refs[:-3], refs[-3:]
        loads = [
            pltpu.make_async_copy(source, table_ref.at[index], sems.at[index])
            for index, source in enumerate((first_ref, second_ref, third_ref))
        ]
        for load in loads:
            load.start()
        weight = (iota((LANES, 256), 0) == 52).astype(F32).astype(BF16)

        def mask(block, carry):
            segments = pl.ds(block * 16, 16)
            rows = pay_ref[segments, :16, :].reshape(256, 256)
            small = pay_ref[segments, 16:24, 128:].astype(F32).reshape(128, LANES)
            early = nn(small.astype(BF16), weight).reshape(16, 8, 256)
            late = nn(pltpu.roll(small, 64, 1).astype(BF16), weight).reshape(16, 8, 256)
            tile = jnp.concatenate([early, late], axis=1).reshape(256, 256)
            place = pl.ds(pl.multiple_of(block * 256, 256), 256)
            for t in range(4):
                lhs_ref[place, t * 256 : (t + 1) * 256] = rows * (tile == float(t)).astype(F32).astype(BF16)
            return carry

        lax.fori_loop(0, 4, mask, 0, unroll=2)
        for load in loads:
            load.wait()
        for half in range(2):
            for index, out, start in jobs[half]:
                source = lhs_ref[half * HALF : (half + 1) * HALF, :]
                outs[out][start : start + HALF, :] = nt(source, table_ref[index]).astype(BF16)

    return run


def late_degrid(payload, tables, jobs, shapes):
    vmem = pl.BlockSpec(memory_space=pltpu.VMEM)
    anywhere = pl.BlockSpec(memory_space=pl.ANY)
    return pl.pallas_call(
        late_kernel(jobs),
        out_shape=shapes,
        in_specs=[vmem, anywhere, anywhere, anywhere],
        out_specs=[vmem] * len(shapes),
        scratch_shapes=[
            pltpu.VMEM((1024, 1024), BF16),
            pltpu.VMEM((3, 256, 1024), BF16),
            pltpu.SemaphoreType.DMA((3,)),
        ],
        compiler_params=SMALL,
        name="late",
    )(payload, *[in_hbm(table) for table in tables])


def payload_kernel(tile_ref, obs_ref, flag_ref, pair_ref, kern_ref, out_ref, kept_ref, stacked_ref, sem):
    bulk = pltpu.make_async_copy(kern_ref.at[:, 16:32, :], out_ref.at[:, 0:16, :], sem)
    bulk.start()
    kept = (1 - flag_ref[...]).astype(F32)
    pair = pair_ref[...]
    high = (pair >> 3).astype(F32)
    low = (pair & 7).astype(F32)
    block = iota((1, ROWS), 1) >> 9
    tile = jnp.where(block < 2, jnp.where(block == 0, tile_ref[0], tile_ref[1]), jnp.where(block == 2, tile_ref[2], tile_ref[3]))
    fill = jnp.zeros((64 - 53, ROWS), F32)
    obs = obs_ref[...].astype(F32)
    stacked_ref[...] = jnp.concatenate([obs[:, 0], obs[:, 1], kept, high, low, tile.astype(F32), fill], axis=0)
    source = iota((64, 256), 0)
    col = iota((64, 256), 1)
    pick = (source == 32 + (col & 15)) & ((col < 32) | (col >= 128))
    pick = pick.astype(F32).astype(BF16)
    rest = (iota((LANES, LANES), 1) >= 32).astype(F32)

    def step(part, carry):
        turned = stacked_ref[:, pl.ds(pl.multiple_of(part * 128, 128), 128)].T
        wide = nn(turned.astype(BF16), pick)
        turned = jnp.concatenate([turned, jnp.zeros((128, 64), F32)], axis=1)
        value = turned * (wide[:, :128] + rest)
        moved = pltpu.roll(value, 64, 1).reshape(4, 4, 8, LANES)
        value = value.reshape(4, 4, 8, LANES)
        segments = pl.ds(part * 4, 4)
        out_ref[segments, 16:24, :128] = (value[:, 0] + moved[:, 1]).astype(BF16)
        out_ref[segments, 16:24, 128:] = (value[:, 2] + moved[:, 3]).astype(BF16)
        kept = wide[:, 128:].reshape(4, 32, LANES)[:, :16].reshape(64, LANES).astype(BF16)
        kept_ref[pl.ds(pl.multiple_of(part * 64, 64), 64), :] = kept
        return carry

    lax.fori_loop(0, ROWS // 128, step, 0, unroll=8)
    bulk.wait()


def make_payload(tile_of, observed, flags, pairs, kernel):
    return pl.pallas_call(
        payload_kernel,
        out_shape=[jax.ShapeDtypeStruct((64, 24, 256), BF16), jax.ShapeDtypeStruct((1024, LANES), BF16)],
        grid_spec=pltpu.PrefetchScalarGridSpec(
            num_scalar_prefetch=1,
            grid=(1,),
            in_specs=[
                full((16, 2, ROWS)),
                full((16, ROWS)),
                full((2, ROWS)),
                pl.BlockSpec(memory_space=pl.ANY),
            ],
            out_specs=[full((64, 24, 256)), full((1024, LANES))],
            scratch_shapes=[pltpu.VMEM((64, ROWS), F32), pltpu.SemaphoreType.DMA],
        ),
        compiler_params=SMALL,
        name="payload",
    )(tile_of, in_hbm(observed), in_hbm(flags), in_hbm(pairs), in_hbm(kernel))


def setup_kernel(pay_ref, order_ref, own_ref, ohq_ref, ohp_ref, opt_ref, vre_ref, vim_ref, kept_ref):
    source = iota((LANES, 5 * LANES), 0)
    col = iota((LANES, 5 * LANES), 1)
    piece = col >> 7
    weight = ((source == 16 * piece + (col & 15)) & (piece < 2)).astype(F32)
    weight = weight + 8.0 * ((source == 49) & (piece == 2)).astype(F32) + ((source == 51) & (piece == 2)).astype(F32)
    weight = weight + 8.0 * ((source == 48) & (piece == 3)).astype(F32) + ((source == 50) & (piece == 3)).astype(F32)
    weight = weight + ((source == 32 + (col & 15)) & (piece == 4)).astype(F32)
    weight = weight.astype(BF16)
    order = order_ref[...]
    own = own_ref[...]

    def step(i, carry):
        value = pay_ref[pl.ds(pl.multiple_of(i * 8, 8), 8), 16:24, :].astype(F32).reshape(64, 256)
        left, right = value[:, :128], value[:, 128:]
        value = jnp.concatenate([left, pltpu.roll(left, 64, 1), right, pltpu.roll(right, 64, 1)], axis=0)
        wide = nn(value.astype(BF16), weight).reshape(4, 8, 8, 5 * LANES)
        for part in range(2):
            rows = pl.ds(pl.multiple_of(i * 128 + part * 1024, 128), 128)
            mine = jnp.concatenate([wide[2 * part], wide[2 * part + 1]], axis=1).reshape(128, 5 * LANES)
            vre_ref[rows, :] = mine[:, :128].astype(BF16)
            vim_ref[rows, :] = mine[:, 128:256].astype(BF16)
            second = mine[:, 256:384]
            for quarter in range(4):
                lanes = slice(quarter * 128, (quarter + 1) * 128)
                ohq_ref[rows, lanes] = (second == order[:, lanes]).astype(F32).astype(BF16)
            near = (mine[:, 384:512] == own).astype(F32)
            ohp_ref[rows, :] = near.astype(BF16)
            opt_ref[:, rows] = near.T[:16, :].astype(BF16)
            if part == 1:
                kept_ref[pl.ds(pl.multiple_of(i * 128, 128), 128), :] = mine[:, 512:].astype(BF16)
        return carry

    lax.fori_loop(0, 8, step, 0)


def make_setup(payload, order, own):
    shapes = [
        pltpu.HBM((ROWS, S), BF16),
        pltpu.HBM((ROWS, LANES), BF16),
        jax.ShapeDtypeStruct((16, ROWS), BF16),
        jax.ShapeDtypeStruct((ROWS, LANES), BF16),
        jax.ShapeDtypeStruct((ROWS, LANES), BF16),
        pltpu.HBM((1024, LANES), BF16),
    ]
    return pl.pallas_call(setup_kernel, out_shape=shapes, compiler_params=SMALL, name="setup")(payload, order, own)


def over_directions(x):
    x = x + pltpu.roll(x, 16, 1)
    x = x + pltpu.roll(x, 32, 1)
    return x + pltpu.roll(x, 64, 1)


def iterate_kernel(first):
    def run(*refs):
        if first:
            model_a, chain_a, chain_b, opt_ref, vre_ref, vim_ref, *sources = refs[:11]
            out_ref, model_b, terms_ref, kept_ref, own_a, own_b, near_a, near_b, sems = refs[11:]
            kept_source, a_source, b_source, low_source, high_source = sources
            moves = [
                (kept_source, kept_ref),
                (a_source, own_a),
                (b_source, own_b),
                (high_source.at[HALF:], near_a),
                (low_source.at[HALF:], near_b),
            ]
            moves = [pltpu.make_async_copy(*move, sems.at[index]) for index, move in enumerate(moves)]
            for move in moves:
                move.start()
        else:
            model_a, model_b, opt_ref, vre_ref, vim_ref, ohq_ref, ohp_ref, here_ref, there_ref, own_ref, out_ref, terms_ref = refs
            all_gains = jnp.concatenate([here_ref[...], there_ref[...]], axis=0)
            own = own_ref[...]
            high = own.astype(BF16).astype(F32)
            near_gains = jnp.concatenate([high, own - high, jnp.zeros((LANES - 16, 256), F32)], axis=0).astype(BF16)

        for i in range(ROWS // CHUNK):
            if first and i == 4:
                for move in moves:
                    move.wait()
                add_kernel(own_a, own_b, chain_a, chain_b, near_a, near_b, kept_ref, model_b)
            rows = slice(i * CHUNK, (i + 1) * CHUNK)
            model = (model_a if i < 4 else model_b)[(i % 4) * CHUNK : (i % 4 + 1) * CHUNK, :].astype(F32)
            model_re, model_im = model[:, :128], model[:, 128:]
            if first:
                prod_re = pred_re = model_re
                prod_im = pred_im = model_im
            else:
                far = nn(ohq_ref[rows, :], all_gains)
                near = nn(ohp_ref[rows, :], near_gains)
                far_re, far_im = far[:, :128], far[:, 128:]
                near_re, near_im = near[:, :128], near[:, 128:]
                prod_re = model_re * far_re + model_im * far_im
                prod_im = model_im * far_re - model_re * far_im
                pred_re = near_re * prod_re - near_im * prod_im
                pred_im = near_re * prod_im + near_im * prod_re
            res_re = vre_ref[rows, :].astype(F32) - over_directions(pred_re)
            res_im = vim_ref[rows, :].astype(F32) - over_directions(pred_im)
            terms = jnp.concatenate(
                [
                    prod_re * res_re + prod_im * res_im,
                    prod_re * res_im - prod_im * res_re,
                    prod_re * prod_re + prod_im * prod_im,
                ],
                axis=1,
            )
            top = terms.astype(BF16)
            terms_ref[rows, :384] = top
            terms_ref[rows, 384:] = (terms - top.astype(F32)).astype(BF16)

        acc = nn(opt_ref[...], terms_ref[...])[:8]
        acc = acc[:, :384] + acc[:, 384:]
        sum_re, sum_im, power = acc[:, :128], acc[:, 128:256], acc[:, 256:]
        if first:
            gain_re = jnp.ones((8, 128), F32)
            gain_im = jnp.zeros((8, 128), F32)
        else:
            gain_re, gain_im = own[:, :128], own[:, 128:]
        new_re = (sum_re + gain_re * power) / (power + 1.0)
        new_im = (sum_im + gain_im * power) / (power + 1.0)
        out_ref[:, :128] = (gain_re + new_re) * 0.5
        out_ref[:, 128:] = (gain_im + new_im) * 0.5

    return run


def iterate(args, first):
    vmem = pl.BlockSpec(memory_space=pltpu.VMEM)
    anywhere = pl.BlockSpec(memory_space=pl.ANY)
    scratch = [pltpu.VMEM((ROWS, 768), BF16)]
    if first:
        scratch += [pltpu.VMEM((1024, LANES), BF16)]
        scratch += [pltpu.VMEM((HALF, 256), BF16)] * 4 + [pltpu.SemaphoreType.DMA((5,))]
    return pl.pallas_call(
        iterate_kernel(first),
        out_shape=[jax.ShapeDtypeStruct((8, 256), F32)] + [jax.ShapeDtypeStruct((1024, 256), BF16)] * first,
        in_specs=[vmem] * 6 + [anywhere] * 5 if first else [vmem] * len(args),
        out_specs=[vmem] * (2 if first else 1),
        scratch_shapes=scratch,
        compiler_params=SMALL,
        name="iterate0" if first else "iterate",
    )(*args)


def smooth_kernel(last):
    def run(where_ref, mid_ref, low_ref, high_ref, *outs):
        chan = iota((8, LANES), 1) & 15
        whole = chan + 16 * where_ref[0]
        has_left = (whole > 0).astype(F32)
        has_right = (whole < 63).astype(F32)
        halves = []
        for part in range(2):
            lanes = slice(part * 128, (part + 1) * 128)
            mid = mid_ref[:, lanes]
            left = jnp.where(chan == 0, pltpu.roll(low_ref[:, lanes], 113, 1), pltpu.roll(mid, 1, 1))
            right = jnp.where(chan == 15, pltpu.roll(high_ref[:, lanes], 15, 1), pltpu.roll(mid, 127, 1))
            total = 0.25 * has_left * left + 0.5 * mid + 0.25 * has_right * right
            halves.append(total / (0.5 + 0.25 * has_left + 0.25 * has_right))
        gains = jnp.concatenate(halves, axis=1)
        if last:
            source = iota((256, 256), 0)
            place = (source & 15) * 16 + ((source >> 4) & 7) * 2 + (source >> 7)
            order = (iota((256, 256), 1) == place).astype(F32)
            gains = jnp.dot(gains, order, precision=lax.Precision.HIGHEST, preferred_element_type=F32)
            for channel in range(16):
                outs[0][channel] = gains[:, channel * 16 : (channel + 1) * 16]
        else:
            outs[0][...] = gains
            outs[1][...] = jnp.broadcast_to(gains.astype(BF16)[None], (32, 8, 256))

    return run


def smooth(where, mid, low, high, last):
    if last:
        shapes = [jax.ShapeDtypeStruct((16, 8, 16), F32)]
    else:
        shapes = [jax.ShapeDtypeStruct((8, 256), F32), jax.ShapeDtypeStruct((32, 8, 256), BF16)]
    smem = pl.BlockSpec(memory_space=pltpu.SMEM)
    vmem = pl.BlockSpec(memory_space=pltpu.VMEM)
    return pl.pallas_call(
        smooth_kernel(last),
        out_shape=shapes,
        in_specs=[smem, vmem, vmem, vmem],
        out_specs=[vmem] * len(shapes),
        compiler_params=SMALL,
        name="finish" if last else "smooth",
    )(where, mid, low, high)


def pair_kernel(left_ref, right_ref, out_ref):
    for part in range(2):
        rows = slice(part * 256, (part + 1) * 256)
        out_ref[rows, :] = (left_ref[rows, :].astype(F32) + right_ref[rows, :].astype(F32)).astype(BF16)


def pair_sum(left, right):
    block = pl.BlockSpec((HALF, 256), lambda i: (0, 0))
    return pl.pallas_call(
        pair_kernel,
        out_shape=jax.ShapeDtypeStruct((HALF, 256), BF16),
        grid=(1,),
        in_specs=[block, block],
        out_specs=block,
        compiler_params=SMALL,
        name="pair",
    )(in_hbm(left) if left.shape[0] > HALF else left, right)


def add_kernel(own_a, own_b, chain_a, chain_b, near_a, near_b, kept_ref, out_ref):
    for half, parts in ((0, (own_a, chain_a, near_a)), (1, (own_b, chain_b, near_b))):
        for part in range(2):
            near = slice(part * 256, (part + 1) * 256)
            rows = slice(half * HALF + part * 256, half * HALF + (part + 1) * 256)
            total = parts[0][near, :].astype(F32) + parts[1][near, :].astype(F32) + parts[2][near, :].astype(F32)
            kept = kept_ref[rows, :].astype(F32)
            out_ref[rows, :128] = (total[:, :128] * kept).astype(BF16)
            out_ref[rows, 128:] = (total[:, 128:] * kept).astype(BF16)


def total(*parts):
    return pl.pallas_call(
        add_kernel, out_shape=jax.ShapeDtypeStruct((1024, 256), BF16), compiler_params=SMALL, name="add"
    )(*parts)


UP = [(i, (i + 1) % 4) for i in range(4)]
DOWN = [(i, (i + 3) % 4) for i in range(4)]


def last_legs(chain_a, chain_b, direct_a, direct_b, next_a, prev_b):
    chain_a = lax.ppermute(pair_sum(chain_a, next_a), "ch", UP)
    chain_b = lax.ppermute(pair_sum(chain_b, prev_b), "ch", DOWN)
    return chain_a, chain_b, direct_a, direct_b


def exchange(value):
    return lax.all_to_all(value, BL, split_axis=0, concat_axis=0, tiled=True)


def body(facet_grid, kernel, tile_of, observed, flags, pairs, solver_order):
    where = lax.axis_index("ch").astype(jnp.int32).reshape(1)
    tile_of = in_hbm(tile_of)
    kernel = kernel.reshape(64, 32, 256)
    payload, kept_a = make_payload(tile_of, observed, flags, pairs, kernel)
    arrived = exchange(payload)

    mine = lax.dynamic_slice(solver_order, (8 * lax.axis_index(BL),), (8,))
    own_row = jnp.concatenate([mine, mine, jnp.full((LANES - 16,), -1, jnp.int32)]).astype(F32).reshape(1, LANES)
    halves = solver_order.reshape(32, 2, 8).transpose(1, 0, 2).astype(F32).reshape(2, S // 2)
    order_row = jnp.where(lax.axis_index("core") == 0, halves, halves[::-1]).reshape(1, S)

    far_a, far_b, table2 = degrid(where, tile_of, kernel, facet_grid, (2,))
    chain_a = lax.ppermute(far_a, "ch", UP)
    chain_b = lax.ppermute(far_b, "ch", DOWN)
    next_a, next_b, prev_a, prev_b, own_a, own_b, table1, table3, table0 = degrid(
        where, tile_of, kernel, facet_grid, (1, 3, 0)
    )
    direct_a = lax.ppermute(prev_a, "ch", DOWN)
    direct_b = lax.ppermute(next_b, "ch", UP)
    legs = last_legs(chain_a, chain_b, direct_a, direct_b, next_a, prev_b)
    model_a = total(own_a, own_b, *legs, kept_a)

    half = jax.ShapeDtypeStruct((HALF, 256), BF16)
    away = pltpu.HBM((HALF, 256), BF16)
    whole = pltpu.HBM((2 * HALF, 256), BF16)
    going_up, going_down = late_degrid(
        arrived,
        (table2, table3, table1),
        (((0, 0, 0), (1, 1, HALF)), ((0, 1, 0), (2, 0, HALF))),
        [whole, whole],
    )
    from_low = lax.ppermute(going_up, "ch", UP)
    from_high = lax.ppermute(going_down, "ch", DOWN)
    next_a, prev_b, own_a, own_b = late_degrid(
        arrived, (table1, table3, table0), (((0, 0, 0), (2, 2, 0)), ((1, 1, 0), (2, 3, 0))), [half, half, away, away]
    )
    ohq, ohp, opt, vis_re, vis_im, kept_b = make_setup(arrived, order_row, own_row)
    chain_a, chain_b, *_ = last_legs(from_low, from_high, None, None, next_a, prev_b)
    model_a = exchange(model_a.reshape(64, 16, 256)).reshape(1024, 256)

    for step in range(ITERS):
        if step == 0:
            sources = map(in_hbm, (kept_b, own_a, own_b, from_low, from_high))
            mid, model_b = iterate((model_a, chain_a, chain_b, opt, vis_re, vis_im, *sources), True)
        else:
            rows = (model_a, model_b, opt, vis_re, vis_im, ohq, ohp)
            both = (everyone.reshape(S // 2, 256), others.reshape(S // 2, 256))
            (mid,) = iterate(rows + both + (gains,), False)
        low = lax.ppermute(mid, "ch", UP)
        high = lax.ppermute(mid, "ch", DOWN)
        if step + 1 < ITERS:
            gains, block = smooth(where, mid, low, high, False)
            everyone = lax.all_to_all(block, ("y", "z"), split_axis=0, concat_axis=0, tiled=True)
            others = lax.ppermute(everyone, "core", [(0, 1), (1, 0)])
        else:
            (gains,) = smooth(where, mid, low, high, True)
    return gains.transpose(0, 2, 1)


def solution(mesh):
    split = Mesh(mesh.devices.reshape(4, 8, 2, 4), BL + ("ch",))
    in_specs = (
        P(None, None, None, "ch"),
        P(BL, "ch"),
        P(BL),
        P("ch", None, BL),
        P("ch", BL),
        P(None, BL),
        P(),
    )
    out_specs = P("ch", None, BL)
    return jax.shard_map(body, mesh=split, in_specs=in_specs, out_specs=out_specs, check_vma=False)
```

```python
import jax
import jax.numpy as jnp
from jax import lax
from jax.experimental import pallas as pl
from jax.experimental.pallas import tpu as pltpu
from jax.sharding import Mesh, PartitionSpec as P

S = 512
ITERS = 4
LANES = 128
ROWS = 2048
HALF = 512
CHUNK = 256
F32 = jnp.float32
BF16 = jnp.bfloat16
BL = ("y", "z", "core")
SMALL = pltpu.CompilerParams(vmem_limit_bytes=16 << 20)


def nt(a, b):
    return lax.dot_general(a, b, (((1,), (1,)), ((), ())), preferred_element_type=F32)


def nn(a, b):
    return lax.dot_general(a, b, (((1,), (0,)), ((), ())), preferred_element_type=F32)


def iota(shape, dim):
    return lax.broadcasted_iota(jnp.int32, shape, dim)


def lane_order():
    lane = iota((256, 256), 0)
    source = (lane & 15) * 16 + ((lane >> 4) & 7) * 2 + (lane >> 7)
    return (iota((256, 256), 1) == source).astype(F32).astype(BF16)


def in_hbm(x):
    return pltpu.with_memory_space_constraint(x, pltpu.HBM)


def full(shape):
    return pl.BlockSpec(shape, lambda i, *scalars: (0,) * len(shape))


def degrid_kernel(count):
    def run(where_ref, tile_ref, kern_ref, *refs):
        facets, outs, tables = refs[:count], refs[count : 3 * count], refs[3 * count : 4 * count]
        order = lane_order()
        for index in range(count):
            for tile in range(4):
                columns = slice(tile * 256, (tile + 1) * 256)
                tables[index][:, columns] = nn(order, facets[index][tile].reshape(256, 256)).astype(BF16)
        for block in range(4):
            rows = kern_ref[block * 16 : (block + 1) * 16].reshape(256, 256)
            place = slice((block % 2) * 256, (block % 2) * 256 + 256)
            columns = pl.ds(pl.multiple_of(tile_ref[block] * 256, 256), 256)
            for index in range(count):
                outs[2 * index + block // 2][place, :] = nt(rows, tables[index][:, columns]).astype(BF16)

    return run


def degrid(where, tile_of, kernel, facet_grid, groups):
    count = len(groups)

    def facet_spec(shift):
        return pl.BlockSpec((4, 16, 16, 256), lambda i, where, tile: (0, (where[0] + shift) & 3, 0, 0))

    half = jax.ShapeDtypeStruct((HALF, 256), BF16)
    table = pltpu.HBM((256, 1024), BF16)
    return pl.pallas_call(
        degrid_kernel(count),
        out_shape=[half] * (2 * count) + [table] * count,
        grid_spec=pltpu.PrefetchScalarGridSpec(
            num_scalar_prefetch=2,
            grid=(1,),
            in_specs=[full((64, 16, 256))] + [facet_spec(g) for g in groups],
            out_specs=[full((HALF, 256))] * (2 * count) + [full((256, 1024))] * count,
        ),
        compiler_params=SMALL,
    )(where, tile_of, in_hbm(kernel), *([in_hbm(facet_grid)] * count))


def late_kernel(jobs, extra):
    def run(pay_ref, first_ref, second_ref, third_ref, *refs):
        arrived, outs, (lhs_ref, table_ref, add_ref, sems) = refs[:extra], refs[extra:-4], refs[-4:]
        loads = [
            pltpu.make_async_copy(source, table_ref.at[index], sems.at[index])
            for index, source in enumerate((first_ref, second_ref, third_ref))
        ]
        loads += [
            pltpu.make_async_copy(source.at[:HALF], add_ref.at[index], sems.at[3 + index])
            for index, source in enumerate(arrived)
        ]
        for load in loads:
            load.start()
        weight = (iota((LANES, 256), 0) == 52).astype(F32).astype(BF16)

        def mask(block, carry):
            segments = pl.ds(block * 16, 16)
            rows = pay_ref[segments, :16, :].reshape(256, 256)
            small = pay_ref[segments, 16:24, 128:].astype(F32).reshape(128, LANES)
            early = nn(small.astype(BF16), weight).reshape(16, 8, 256)
            late = nn(pltpu.roll(small, 64, 1).astype(BF16), weight).reshape(16, 8, 256)
            tile = jnp.concatenate([early, late], axis=1).reshape(256, 256)
            place = pl.ds(pl.multiple_of(block * 256, 256), 256)
            for t in range(4):
                lhs_ref[place, t * 256 : (t + 1) * 256] = rows * (tile == float(t)).astype(F32).astype(BF16)
            return carry

        lax.fori_loop(0, 4, mask, 0, unroll=2)
        for load in loads:
            load.wait()
        for half in range(2):
            for index, out, start in jobs[half]:
                source = lhs_ref[half * HALF : (half + 1) * HALF, :]
                value = nt(source, table_ref[index])
                if out < extra:
                    value = value + add_ref[out].astype(F32)
                outs[out][start : start + HALF, :] = value.astype(BF16)

    return run


def late_degrid(payload, tables, jobs, shapes, arrived=()):
    vmem = pl.BlockSpec(memory_space=pltpu.VMEM)
    anywhere = pl.BlockSpec(memory_space=pl.ANY)
    return pl.pallas_call(
        late_kernel(jobs, len(arrived)),
        out_shape=shapes,
        in_specs=[vmem] + [anywhere] * (3 + len(arrived)),
        out_specs=[vmem] * len(shapes),
        scratch_shapes=[
            pltpu.VMEM((1024, 1024), BF16),
            pltpu.VMEM((3, 256, 1024), BF16),
            pltpu.VMEM((2, HALF, 256), BF16),
            pltpu.SemaphoreType.DMA((5,)),
        ],
        compiler_params=SMALL,
        name="late",
    )(payload, *[in_hbm(item) for item in (*tables, *arrived)])


def payload_kernel(tile_ref, obs_ref, flag_ref, pair_ref, kern_ref, out_ref, kept_ref, stacked_ref, sem):
    bulk = pltpu.make_async_copy(kern_ref.at[:, 16:32, :], out_ref.at[:, 0:16, :], sem)
    bulk.start()
    kept = (1 - flag_ref[...]).astype(F32)
    pair = pair_ref[...]
    high = (pair >> 3).astype(F32)
    low = (pair & 7).astype(F32)
    block = iota((1, ROWS), 1) >> 9
    tile = jnp.where(block < 2, jnp.where(block == 0, tile_ref[0], tile_ref[1]), jnp.where(block == 2, tile_ref[2], tile_ref[3]))
    fill = jnp.zeros((64 - 53, ROWS), F32)
    obs = obs_ref[...].astype(F32)
    stacked_ref[...] = jnp.concatenate([obs[:, 0], obs[:, 1], kept, high, low, tile.astype(F32), fill], axis=0)
    source = iota((64, 256), 0)
    col = iota((64, 256), 1)
    pick = (source == 32 + (col & 15)) & ((col < 32) | (col >= 128))
    pick = pick.astype(F32).astype(BF16)
    rest = (iota((LANES, LANES), 1) >= 32).astype(F32)

    def step(part, carry):
        turned = stacked_ref[:, pl.ds(pl.multiple_of(part * 128, 128), 128)].T
        wide = nn(turned.astype(BF16), pick)
        turned = jnp.concatenate([turned, jnp.zeros((128, 64), F32)], axis=1)
        value = turned * (wide[:, :128] + rest)
        moved = pltpu.roll(value, 64, 1).reshape(4, 4, 8, LANES)
        value = value.reshape(4, 4, 8, LANES)
        segments = pl.ds(part * 4, 4)
        out_ref[segments, 16:24, :128] = (value[:, 0] + moved[:, 1]).astype(BF16)
        out_ref[segments, 16:24, 128:] = (value[:, 2] + moved[:, 3]).astype(BF16)
        kept = wide[:, 128:].reshape(4, 32, LANES)[:, :16].reshape(64, LANES).astype(BF16)
        kept_ref[pl.ds(pl.multiple_of(part * 64, 64), 64), :] = kept
        return carry

    lax.fori_loop(0, ROWS // 128, step, 0, unroll=8)
    bulk.wait()


def make_payload(tile_of, observed, flags, pairs, kernel):
    return pl.pallas_call(
        payload_kernel,
        out_shape=[jax.ShapeDtypeStruct((64, 24, 256), BF16), jax.ShapeDtypeStruct((1024, LANES), BF16)],
        grid_spec=pltpu.PrefetchScalarGridSpec(
            num_scalar_prefetch=1,
            grid=(1,),
            in_specs=[
                full((16, 2, ROWS)),
                full((16, ROWS)),
                full((2, ROWS)),
                pl.BlockSpec(memory_space=pl.ANY),
            ],
            out_specs=[full((64, 24, 256)), full((1024, LANES))],
            scratch_shapes=[pltpu.VMEM((64, ROWS), F32), pltpu.SemaphoreType.DMA],
        ),
        compiler_params=SMALL,
        name="payload",
    )(tile_of, in_hbm(observed), in_hbm(flags), in_hbm(pairs), in_hbm(kernel))


def setup_kernel(pay_ref, order_ref, own_ref, ohq_ref, ohp_ref, opt_ref, vre_ref, vim_ref, kept_ref):
    source = iota((LANES, 5 * LANES), 0)
    col = iota((LANES, 5 * LANES), 1)
    piece = col >> 7
    weight = ((source == 16 * piece + (col & 15)) & (piece < 2)).astype(F32)
    weight = weight + 8.0 * ((source == 49) & (piece == 2)).astype(F32) + ((source == 51) & (piece == 2)).astype(F32)
    weight = weight + 8.0 * ((source == 48) & (piece == 3)).astype(F32) + ((source == 50) & (piece == 3)).astype(F32)
    weight = weight + ((source == 32 + (col & 15)) & (piece == 4)).astype(F32)
    weight = weight.astype(BF16)
    order = order_ref[...]
    own = own_ref[...]

    def step(i, carry):
        value = pay_ref[pl.ds(pl.multiple_of(i * 8, 8), 8), 16:24, :].astype(F32).reshape(64, 256)
        left, right = value[:, :128], value[:, 128:]
        value = jnp.concatenate([left, pltpu.roll(left, 64, 1), right, pltpu.roll(right, 64, 1)], axis=0)
        wide = nn(value.astype(BF16), weight).reshape(4, 8, 8, 5 * LANES)
        for part in range(2):
            rows = pl.ds(pl.multiple_of(i * 128 + part * 1024, 128), 128)
            mine = jnp.concatenate([wide[2 * part], wide[2 * part + 1]], axis=1).reshape(128, 5 * LANES)
            vre_ref[rows, :] = mine[:, :128].astype(BF16)
            vim_ref[rows, :] = mine[:, 128:256].astype(BF16)
            second = mine[:, 256:384]
            for quarter in range(4):
                lanes = slice(quarter * 128, (quarter + 1) * 128)
                ohq_ref[rows, lanes] = (second == order[:, lanes]).astype(F32).astype(BF16)
            near = (mine[:, 384:512] == own).astype(F32)
            ohp_ref[rows, :] = near.astype(BF16)
            opt_ref[:, rows] = near.T[:16, :].astype(BF16)
            if part == 1:
                kept_ref[pl.ds(pl.multiple_of(i * 128, 128), 128), :] = mine[:, 512:].astype(BF16)
        return carry

    lax.fori_loop(0, 8, step, 0)


def make_setup(payload, order, own):
    shapes = [
        pltpu.HBM((ROWS, S), BF16),
        pltpu.HBM((ROWS, LANES), BF16),
        jax.ShapeDtypeStruct((16, ROWS), BF16),
        jax.ShapeDtypeStruct((ROWS, LANES), BF16),
        jax.ShapeDtypeStruct((ROWS, LANES), BF16),
        pltpu.HBM((1024, LANES), BF16),
    ]
    return pl.pallas_call(setup_kernel, out_shape=shapes, compiler_params=SMALL, name="setup")(payload, order, own)


def over_directions(x):
    x = x + pltpu.roll(x, 16, 1)
    x = x + pltpu.roll(x, 32, 1)
    return x + pltpu.roll(x, 64, 1)


def iterate_kernel(first):
    def run(*refs):
        if first:
            model_a, chain_a, chain_b, opt_ref, vre_ref, vim_ref, *sources = refs[:11]
            out_ref, model_b, terms_ref, kept_ref, own_a, own_b, near_a, near_b, sems = refs[11:]
            kept_source, a_source, b_source, low_source, high_source = sources
            moves = [
                (kept_source, kept_ref),
                (a_source, own_a),
                (b_source, own_b),
                (high_source.at[HALF:], near_a),
                (low_source.at[HALF:], near_b),
            ]
            moves = [pltpu.make_async_copy(*move, sems.at[index]) for index, move in enumerate(moves)]
            for move in moves:
                move.start()
        else:
            model_a, model_b, opt_ref, vre_ref, vim_ref, ohq_ref, ohp_ref, here_ref, there_ref, own_ref, out_ref, terms_ref = refs
            all_gains = jnp.concatenate([here_ref[...], there_ref[...]], axis=0)
            own = own_ref[...]
            high = own.astype(BF16).astype(F32)
            near_gains = jnp.concatenate([high, own - high, jnp.zeros((LANES - 16, 256), F32)], axis=0).astype(BF16)

        for i in range(ROWS // CHUNK):
            if first and i == 4:
                for move in moves:
                    move.wait()
                add_kernel(own_a, own_b, chain_a, chain_b, near_a, near_b, kept_ref, model_b)
            rows = slice(i * CHUNK, (i + 1) * CHUNK)
            model = (model_a if i < 4 else model_b)[(i % 4) * CHUNK : (i % 4 + 1) * CHUNK, :].astype(F32)
            model_re, model_im = model[:, :128], model[:, 128:]
            if first:
                prod_re = pred_re = model_re
                prod_im = pred_im = model_im
            else:
                far = nn(ohq_ref[rows, :], all_gains)
                near = nn(ohp_ref[rows, :], near_gains)
                far_re, far_im = far[:, :128], far[:, 128:]
                near_re, near_im = near[:, :128], near[:, 128:]
                prod_re = model_re * far_re + model_im * far_im
                prod_im = model_im * far_re - model_re * far_im
                pred_re = near_re * prod_re - near_im * prod_im
                pred_im = near_re * prod_im + near_im * prod_re
            res_re = vre_ref[rows, :].astype(F32) - over_directions(pred_re)
            res_im = vim_ref[rows, :].astype(F32) - over_directions(pred_im)
            terms = jnp.concatenate(
                [
                    prod_re * res_re + prod_im * res_im,
                    prod_re * res_im - prod_im * res_re,
                    prod_re * prod_re + prod_im * prod_im,
                ],
                axis=1,
            )
            top = terms.astype(BF16)
            terms_ref[rows, :384] = top
            terms_ref[rows, 384:] = (terms - top.astype(F32)).astype(BF16)

        acc = nn(opt_ref[...], terms_ref[...])[:8]
        acc = acc[:, :384] + acc[:, 384:]
        sum_re, sum_im, power = acc[:, :128], acc[:, 128:256], acc[:, 256:]
        if first:
            gain_re = jnp.ones((8, 128), F32)
            gain_im = jnp.zeros((8, 128), F32)
        else:
            gain_re, gain_im = own[:, :128], own[:, 128:]
        new_re = (sum_re + gain_re * power) / (power + 1.0)
        new_im = (sum_im + gain_im * power) / (power + 1.0)
        out_ref[:, :128] = (gain_re + new_re) * 0.5
        out_ref[:, 128:] = (gain_im + new_im) * 0.5

    return run


def iterate(args, first):
    vmem = pl.BlockSpec(memory_space=pltpu.VMEM)
    anywhere = pl.BlockSpec(memory_space=pl.ANY)
    scratch = [pltpu.VMEM((ROWS, 768), BF16)]
    if first:
        scratch += [pltpu.VMEM((1024, LANES), BF16)]
        scratch += [pltpu.VMEM((HALF, 256), BF16)] * 4 + [pltpu.SemaphoreType.DMA((5,))]
    return pl.pallas_call(
        iterate_kernel(first),
        out_shape=[jax.ShapeDtypeStruct((8, 256), F32)] + [jax.ShapeDtypeStruct((1024, 256), BF16)] * first,
        in_specs=[vmem] * 6 + [anywhere] * 5 if first else [vmem] * len(args),
        out_specs=[vmem] * (2 if first else 1),
        scratch_shapes=scratch,
        compiler_params=SMALL,
        name="iterate0" if first else "iterate",
    )(*args)


def smooth_kernel(last):
    def run(where_ref, mid_ref, low_ref, high_ref, *outs):
        chan = iota((8, LANES), 1) & 15
        whole = chan + 16 * where_ref[0]
        has_left = (whole > 0).astype(F32)
        has_right = (whole < 63).astype(F32)
        halves = []
        for part in range(2):
            lanes = slice(part * 128, (part + 1) * 128)
            mid = mid_ref[:, lanes]
            left = jnp.where(chan == 0, pltpu.roll(low_ref[:, lanes], 113, 1), pltpu.roll(mid, 1, 1))
            right = jnp.where(chan == 15, pltpu.roll(high_ref[:, lanes], 15, 1), pltpu.roll(mid, 127, 1))
            total = 0.25 * has_left * left + 0.5 * mid + 0.25 * has_right * right
            halves.append(total / (0.5 + 0.25 * has_left + 0.25 * has_right))
        gains = jnp.concatenate(halves, axis=1)
        if last:
            source = iota((256, 256), 0)
            place = (source & 15) * 16 + ((source >> 4) & 7) * 2 + (source >> 7)
            order = (iota((256, 256), 1) == place).astype(F32)
            gains = jnp.dot(gains, order, precision=lax.Precision.HIGHEST, preferred_element_type=F32)
            for channel in range(16):
                outs[0][channel] = gains[:, channel * 16 : (channel + 1) * 16]
        else:
            outs[0][...] = gains
            outs[1][...] = jnp.broadcast_to(gains.astype(BF16)[None], (32, 8, 256))

    return run


def smooth(where, mid, low, high, last):
    if last:
        shapes = [jax.ShapeDtypeStruct((16, 8, 16), F32)]
    else:
        shapes = [jax.ShapeDtypeStruct((8, 256), F32), jax.ShapeDtypeStruct((32, 8, 256), BF16)]
    smem = pl.BlockSpec(memory_space=pltpu.SMEM)
    vmem = pl.BlockSpec(memory_space=pltpu.VMEM)
    return pl.pallas_call(
        smooth_kernel(last),
        out_shape=shapes,
        in_specs=[smem, vmem, vmem, vmem],
        out_specs=[vmem] * len(shapes),
        compiler_params=SMALL,
        name="finish" if last else "smooth",
    )(where, mid, low, high)


def pair_kernel(left_ref, right_ref, out_ref):
    for part in range(2):
        rows = slice(part * 256, (part + 1) * 256)
        out_ref[rows, :] = (left_ref[rows, :].astype(F32) + right_ref[rows, :].astype(F32)).astype(BF16)


def pair_sum(left, right):
    block = pl.BlockSpec((HALF, 256), lambda i: (0, 0))
    return pl.pallas_call(
        pair_kernel,
        out_shape=jax.ShapeDtypeStruct((HALF, 256), BF16),
        grid=(1,),
        in_specs=[block, block],
        out_specs=block,
        compiler_params=SMALL,
        name="pair",
    )(in_hbm(left) if left.shape[0] > HALF else left, right)


def add_kernel(own_a, own_b, chain_a, chain_b, near_a, near_b, kept_ref, out_ref):
    for half, parts in ((0, (own_a, chain_a, near_a)), (1, (own_b, chain_b, near_b))):
        for part in range(2):
            near = slice(part * 256, (part + 1) * 256)
            rows = slice(half * HALF + part * 256, half * HALF + (part + 1) * 256)
            total = parts[0][near, :].astype(F32) + parts[1][near, :].astype(F32) + parts[2][near, :].astype(F32)
            kept = kept_ref[rows, :].astype(F32)
            out_ref[rows, :128] = (total[:, :128] * kept).astype(BF16)
            out_ref[rows, 128:] = (total[:, 128:] * kept).astype(BF16)


def total(*parts):
    return pl.pallas_call(
        add_kernel, out_shape=jax.ShapeDtypeStruct((1024, 256), BF16), compiler_params=SMALL, name="add"
    )(*parts)


UP = [(i, (i + 1) % 4) for i in range(4)]
DOWN = [(i, (i + 3) % 4) for i in range(4)]


def last_legs(chain_a, chain_b, direct_a, direct_b, next_a, prev_b):
    chain_a = lax.ppermute(pair_sum(chain_a, next_a), "ch", UP)
    chain_b = lax.ppermute(pair_sum(chain_b, prev_b), "ch", DOWN)
    return chain_a, chain_b, direct_a, direct_b


def exchange(value):
    return lax.all_to_all(value, BL, split_axis=0, concat_axis=0, tiled=True)


def body(facet_grid, kernel, tile_of, observed, flags, pairs, solver_order):
    where = lax.axis_index("ch").astype(jnp.int32).reshape(1)
    tile_of = in_hbm(tile_of)
    kernel = kernel.reshape(64, 32, 256)
    payload, kept_a = make_payload(tile_of, observed, flags, pairs, kernel)
    arrived = exchange(payload)

    mine = lax.dynamic_slice(solver_order, (8 * lax.axis_index(BL),), (8,))
    own_row = jnp.concatenate([mine, mine, jnp.full((LANES - 16,), -1, jnp.int32)]).astype(F32).reshape(1, LANES)
    halves = solver_order.reshape(32, 2, 8).transpose(1, 0, 2).astype(F32).reshape(2, S // 2)
    order_row = jnp.where(lax.axis_index("core") == 0, halves, halves[::-1]).reshape(1, S)

    far_a, far_b, table2 = degrid(where, tile_of, kernel, facet_grid, (2,))
    chain_a = lax.ppermute(far_a, "ch", UP)
    chain_b = lax.ppermute(far_b, "ch", DOWN)
    next_a, next_b, prev_a, prev_b, own_a, own_b, table1, table3, table0 = degrid(
        where, tile_of, kernel, facet_grid, (1, 3, 0)
    )
    direct_a = lax.ppermute(prev_a, "ch", DOWN)
    direct_b = lax.ppermute(next_b, "ch", UP)
    legs = last_legs(chain_a, chain_b, direct_a, direct_b, next_a, prev_b)
    model_a = total(own_a, own_b, *legs, kept_a)

    half = jax.ShapeDtypeStruct((HALF, 256), BF16)
    away = pltpu.HBM((HALF, 256), BF16)
    whole = pltpu.HBM((2 * HALF, 256), BF16)
    going_up, going_down = late_degrid(
        arrived,
        (table2, table3, table1),
        (((0, 0, 0), (1, 1, HALF)), ((0, 1, 0), (2, 0, HALF))),
        [whole, whole],
    )
    from_low = lax.ppermute(going_up, "ch", UP)
    from_high = lax.ppermute(going_down, "ch", DOWN)
    sum_a, sum_b, own_a, own_b = late_degrid(
        arrived,
        (table1, table3, table0),
        (((0, 0, 0), (2, 2, 0)), ((1, 1, 0), (2, 3, 0))),
        [half, half, away, away],
        (from_low, from_high),
    )
    ohq, ohp, opt, vis_re, vis_im, kept_b = make_setup(arrived, order_row, own_row)
    chain_a = lax.ppermute(sum_a, "ch", UP)
    chain_b = lax.ppermute(sum_b, "ch", DOWN)
    model_a = exchange(model_a.reshape(64, 16, 256)).reshape(1024, 256)

    for step in range(ITERS):
        if step == 0:
            sources = map(in_hbm, (kept_b, own_a, own_b, from_low, from_high))
            mid, model_b = iterate((model_a, chain_a, chain_b, opt, vis_re, vis_im, *sources), True)
        else:
            rows = (model_a, model_b, opt, vis_re, vis_im, ohq, ohp)
            both = (everyone.reshape(S // 2, 256), others.reshape(S // 2, 256))
            (mid,) = iterate(rows + both + (gains,), False)
        low = lax.ppermute(mid, "ch", UP)
        high = lax.ppermute(mid, "ch", DOWN)
        if step + 1 < ITERS:
            gains, block = smooth(where, mid, low, high, False)
            everyone = lax.all_to_all(block, ("y", "z"), split_axis=0, concat_axis=0, tiled=True)
            others = lax.ppermute(everyone, "core", [(0, 1), (1, 0)])
        else:
            (gains,) = smooth(where, mid, low, high, True)
    return gains.transpose(0, 2, 1)


def solution(mesh):
    split = Mesh(mesh.devices.reshape(4, 8, 2, 4), BL + ("ch",))
    in_specs = (
        P(None, None, None, "ch"),
        P(BL, "ch"),
        P(BL),
        P("ch", None, BL),
        P("ch", BL),
        P(None, BL),
        P(),
    )
    out_specs = P("ch", None, BL)
    return jax.shard_map(body, mesh=split, in_specs=in_specs, out_specs=out_specs, check_vma=False)
```
